128 devices in a mesh: dp: 4 (over x), tensor: 32 (over y, z, core).
Axes of the slice: x: 4, y: 4, z: 4, core: 2. Of those that a mesh axis runs over, the one named last changes fastest.
Arguments:
- tokens: bfloat16 [16384, 2048], P(('dp', 'tensor')), may hold values from -6 to 6
- norm_gain: bfloat16 [2048], replicated, may hold values from 0.099609375 to 1.8984375
- routes: int32 [16384, 6], P(('dp', 'tensor')), may hold values from 0 to 31, all different within a row; in each aligned block of 128 rows (0 to 127, 128 to 255, ...) at most 32 rows name the same one
- route_gates: bfloat16 [16384, 6], P(('dp', 'tensor')), may hold values from 0.19921875 to 1
- lengths: int32 [24], replicated, may hold values from 1 to 1920, 16384 in all
- request_adapter: int32 [24], replicated, may hold values from 0 to 31
- adapter_slot: int32 [32], replicated, may hold values from 0 to 31, each once
- expert_gate: bfloat16 [32, 2048, 1408], P('tensor'), may hold values from -0.125 to 0.125
- expert_up: bfloat16 [32, 2048, 1408], P('tensor'), may hold values from -0.125 to 0.125
- expert_down: bfloat16 [32, 1408, 2048], P('tensor'), may hold values from -0.15625 to 0.15625
- shared_gate: bfloat16 [2048, 1408], P(None, 'dp'), may hold values from -0.125 to 0.125
- shared_up_weight: bfloat16 [2048, 1408], P(None, 'dp'), may hold values from -0.125 to 0.125
- shared_down: bfloat16 [1408, 2048], P('dp'), may hold values from -0.15625 to 0.15625
- adapter_down: bfloat16 [32, 2048, 16], P('dp'), may hold values from -0.125 to 0.125
- adapter_up: bfloat16 [32, 16, 2048], P('dp'), may hold values from -1.5 to 1.5
- head_weight: bfloat16 [2048, 65536], P(None, ('dp', 'tensor')), may hold values from -0.375 to 0.375
Outputs:
- sublayer_out: bfloat16 [16384, 2048], P(('dp', 'tensor'))
- last_norm: float32 [24], replicated
- block_logit: float32 [24, 32], P(None, 'tensor')
The draws below stay inside these ranges and needn't reach their ends.
Inputs may be any that keep to these rules, and one draw needn't show every extreme that they name: `routes`: in each aligned block of 128 rows (the rows of one device), no expert is named by more than 32 rows, a bound that some block reaches. The lengths sum to 16384; the largest is exactly 1920. Each position of the store appears once: adapter a is stored at position adapter_slot[a] of adapter_down and adapter_up.
All inputs are finite; a program needn't handle non-finite values.
Results may differ from the reference program's by a relative error of at most 0.0066.
Values may be sent and summed in bfloat16 or wider, within the bound.
A program may use at most 128 MiB of HBM per device.

```python
import math
import jax
import jax.numpy as jnp
import numpy as np
from jax import lax

D = 2048
FF = 1408
SFF = 1408
EXPERTS = 32
TOP = 6
RANK = 16
ADAPTERS = 32
VOCAB = 65536
REQUESTS = 24
TOK_DEV = 128
TOKENS = 16384
CAP = 32
LONGEST_LENGTH = 1920
N_DP = 4
N_TENSOR = 32
DEVICES = 128


def set_ends(values, own_key, smallest, largest):
    extent = values.shape
    index_at = [jax.random.randint(jax.random.fold_in(own_key, axis), (), 0, extent[axis]) for axis in range(len(extent))]
    values = values.at[tuple(index_at)].set(smallest)
    longest = extent.index(max(extent))
    index_at[longest] = (index_at[longest] + 1) % extent[longest]
    return values.at[tuple(index_at)].set(largest)


def block_levels(key, shape, split, smallest, top_value):
    def one(axis_at, parts):
        steps = jax.random.uniform(jax.random.fold_in(jax.random.fold_in(key, 6), axis_at), (parts,), jnp.float32, smallest / len(split), top_value / len(split))
        return jnp.repeat(jnp.exp(steps), shape[axis_at] // parts).reshape((-1,) + (1,) * (len(shape) - axis_at - 1))

    gain = one(*split[0])
    for cut in split[1:]:
        gain = gain * one(*cut)
    return gain


def cumulative_ranks(amount, skew):
    loads = [(1 << 20) // math.isqrt(rank ** skew) + 1 for rank in range(1, amount + 1)]
    deviation = 1 + sum(loads) // (1 << 30)
    return np.cumsum(np.array([max(1, weight // deviation) for weight in loads]))


def skewed_ids(stream_key, shape, amount, lean):
    grid = cumulative_ranks(amount, lean)
    pick = jax.random.randint(jax.random.fold_in(stream_key, 1), shape, 0, int(grid[amount - 1]))
    grade = jnp.searchsorted(jnp.asarray(grid, jnp.int32), pick, side="right")
    return jax.random.permutation(jax.random.fold_in(stream_key, 2), amount)[grade].astype(jnp.int32)


def split_up(number_of, total, bound, slope):
    loads = [(1 << 20) // math.isqrt(standing ** slope) + 1 for standing in range(2, number_of + 1)]
    rest, counts = total - bound - (number_of - 1), [1] * (number_of - 1)
    while rest > 0:
        movable = [i for i in range(number_of - 1) if counts[i] < bound]
        whole, remaining = sum([loads[i] for i in movable]), rest
        for i in movable:
            more = min(bound - counts[i], max(1, remaining * loads[i] // whole), rest)
            counts[i] = counts[i] + more
            rest = rest - more
    return np.array([bound] + counts)


def ragged_sizes(rng, amount, total, reach, skew):
    if amount == 2:
        one = jax.random.randint(rng, (), max(1, total - reach), min(reach, total - 1) + 1)
        return jnp.stack([one, total - one])
    sizes = jnp.asarray(split_up(amount, total, reach, skew), jnp.int32)
    twos = (amount - 1) // 2
    giver, taker = sizes[1:1 + 2 * twos:2], sizes[2:2 + 2 * twos:2]
    room = jnp.minimum(giver - 1, reach - taker)
    passed = jax.random.randint(jax.random.fold_in(rng, 1), (twos,), 0, 1 << 20) % (room + 1)
    sizes = sizes.at[1:1 + 2 * twos:2].set(giver - passed).at[2:2 + 2 * twos:2].set(taker + passed)
    return sizes[jax.random.permutation(jax.random.fold_in(rng, 2), amount)]


def deal_out(own_key, own, number, rows, number_of, top, limit, lean):
    sequence = jax.random.permutation(own_key, number_of)
    packed, usual = shares(number_of, rows * top, limit, lean, True), shares(number_of, rows * top, limit, lean, False)
    places = jnp.arange(number_of)

    def named(sizes, rotation):
        used = int((sizes > 0).sum())
        fixed = max(1, used // 4)
        shifted = fixed + (places - fixed + rotation * (used - fixed)) % max(1, number_of - fixed)
        return jnp.zeros((number_of,), jnp.int32).at[sequence[jnp.where(places < fixed, places, shifted)]].set(jnp.asarray(sizes, jnp.int32))

    sizes = jnp.where(number % 4 == 0, named(packed, number // 4), named(usual, number - number // 4 - 1))
    mixed = jax.random.permutation(jax.random.fold_in(own, 3), number_of)
    source_of, sink = mixed[0:number_of // 2 * 2:2], mixed[1:number_of // 2 * 2:2]
    margin = jnp.minimum(sizes[source_of] - 1, limit - sizes[sink]) // 2
    margin = jnp.where((source_of == sequence[0]) | (sink == sequence[0]) | (sizes[sink] == 0), 0, jnp.maximum(margin, 0))
    shifted = jax.random.randint(jax.random.fold_in(own, 4), (number_of // 2,), 0, 1 << 20) % (margin + 1)
    sizes = sizes.at[source_of].add(-shifted).at[sink].add(shifted)
    items = jnp.searchsorted(jnp.cumsum(sizes), jnp.arange(rows * top), side="right").astype(jnp.int32)
    table = items.reshape(top, rows).T
    table = table[jax.random.permutation(jax.random.fold_in(own, 1), rows)]
    rotation = jax.random.randint(jax.random.fold_in(own, 2), (rows, 1), 0, top)
    return jnp.take_along_axis(table, (jnp.arange(top)[None, :] + rotation) % top, axis=1)


def shares(count, total, reach, lean, full):
    weights = [(1 << 20) // math.isqrt(grade ** lean) + 1 for grade in range(1, count + 1)]
    largest = reach if full else min(reach, max(-(-total // count), total * weights[0] // sum(weights)))
    least = 1 if total - largest >= count - 1 else 0
    given, spare = [largest] + [least] * (count - 1), total - largest - least * (count - 1)
    while spare > 0:
        free = [i for i in range(1, count) if given[i] < largest] or [i for i in range(1, count) if given[i] < reach]
        mass, remaining = sum([weights[i] for i in free]), spare
        for i in free:
            addition = min(reach - given[i], max(1, remaining * weights[i] // mass), spare)
            given[i] = given[i] + addition
            spare = spare - addition
    return np.array(given)


def normal_values(key, extent, deviation, most, pieces=(), kind=jnp.bfloat16):
    values = deviation * jax.random.normal(key, extent, jnp.float32)
    if pieces:
        values = values * block_levels(key, extent, pieces, -0.22, 0.18)
    return jnp.clip(values, -most, most).astype(kind)


def setup_inputs(seed: int = 0) -> dict:
    seeds = jax.random.split(jax.random.key(seed), 17)
    tokens = normal_values(seeds[0], (TOKENS, D), 1.0, 6.0, ((0, 128),))
    norm_gain = jnp.clip(1.0 + 0.18 * jax.random.normal(seeds[1], (D,), jnp.float32), 0.099609375, 1.8984375).astype(jnp.bfloat16)
    routes_keys = jax.random.split(jax.random.fold_in(seeds[2], 1), TOKENS // TOK_DEV)
    routes_turns = jax.random.permutation(jax.random.fold_in(seeds[2], 3), TOKENS // TOK_DEV)
    routes = jax.vmap(lambda own, number: deal_out(jax.random.fold_in(seeds[2], 2), own, number, TOK_DEV, EXPERTS, TOP, CAP, 2))(routes_keys, routes_turns).reshape((TOKENS, TOP))
    route_gates = jnp.clip(0.19921875 + 0.80078125 * jax.random.uniform(seeds[3], (TOKENS, TOP), jnp.float32) ** block_levels(seeds[3], (TOKENS, TOP), ((0, 128),), -0.2, 0.2), 0.19921875, 1.0).astype(jnp.bfloat16)
    lengths = ragged_sizes(seeds[4], REQUESTS, TOKENS, LONGEST_LENGTH, 2).astype(jnp.int32)
    request_adapter = set_ends(skewed_ids(seeds[5], (REQUESTS,), ADAPTERS, 2), jax.random.fold_in(seeds[5], 3), 0, ADAPTERS - 1).astype(jnp.int32)
    adapter_slot = jax.random.permutation(seeds[6], ADAPTERS).astype(jnp.int32)
    expert_gate = normal_values(seeds[7], (EXPERTS, D, FF), D ** -0.5, 0.125, ((0, 32),))
    expert_up = normal_values(seeds[8], (EXPERTS, D, FF), D ** -0.5, 0.125, ((0, 32),))
    expert_down = normal_values(seeds[9], (EXPERTS, FF, D), FF ** -0.5, 0.15625, ((0, 32),))
    shared_gate = normal_values(seeds[10], (D, SFF), D ** -0.5, 0.125, ((1, 4),))
    shared_up_weight = normal_values(seeds[11], (D, SFF), D ** -0.5, 0.125, ((1, 4),))
    shared_down = normal_values(seeds[12], (SFF, D), SFF ** -0.5, 0.15625, ((0, 4),))
    adapter_down = normal_values(seeds[13], (ADAPTERS, D, RANK), D ** -0.5, 0.125, ((0, 4),))
    adapter_up = normal_values(seeds[14], (ADAPTERS, RANK, D), RANK ** -0.5, 1.5, ((0, 4),))
    head_weight = normal_values(seeds[15], (D, VOCAB), (D // 9) ** -0.5, 0.375, ((1, 128),))
    return {"tokens": tokens, "norm_gain": norm_gain, "routes": routes, "route_gates": route_gates, "lengths": lengths, "request_adapter": request_adapter, "adapter_slot": adapter_slot, "expert_gate": expert_gate, "expert_up": expert_up, "expert_down": expert_down, "shared_gate": shared_gate, "shared_up_weight": shared_up_weight, "shared_down": shared_down, "adapter_down": adapter_down, "adapter_up": adapter_up, "head_weight": head_weight}


def apply_norm(tokens, norm_gain):
    values = tokens.astype(jnp.float32)
    scaled = lax.rsqrt(lax.optimization_barrier(jnp.mean(values * values, axis=-1, keepdims=True)) + 1e-06)
    return (values * scaled * norm_gain.astype(jnp.float32)).astype(jnp.bfloat16)

def feed_forward(inputs, gate_mat, up_mat, down_mat):
    gate_portion = jnp.dot(inputs, gate_mat, preferred_element_type=jnp.float32)
    up_part = jnp.dot(inputs, up_mat, preferred_element_type=jnp.float32)
    hidden = (jax.nn.silu(gate_portion) * up_part).astype(jnp.bfloat16)
    return jnp.dot(hidden, down_mat, preferred_element_type=jnp.float32)

def token_slots(positions, lengths, request_adapter, adapter_slot):
    request_ends = jnp.cumsum(lengths).astype(jnp.int32)
    request = lax.optimization_barrier(jnp.sum((request_ends[None, :] <= positions[:, None]).astype(jnp.int32), axis=1)).astype(jnp.int32)
    request_pick = request[:, None] == jnp.arange(request_adapter.shape[0], dtype=jnp.int32)[None, :]
    adapter = lax.optimization_barrier(jnp.sum(jnp.where(request_pick, request_adapter[None, :], 0), axis=1)).astype(jnp.int32)
    adapter_pick = adapter[:, None] == jnp.arange(adapter_slot.shape[0], dtype=jnp.int32)[None, :]
    return lax.optimization_barrier(jnp.sum(jnp.where(adapter_pick, adapter_slot[None, :], 0), axis=1)).astype(jnp.int32)

def adapter_delta(inputs, slot_ids, down_store, up_store, first_slot):
    held_count = down_store.shape[0]
    model_width = down_store.shape[1]
    rank_size = down_store.shape[2]
    flat_down = jnp.transpose(down_store, (1, 0, 2)).reshape(model_width, held_count * rank_size)
    low_rank = jnp.dot(inputs, flat_down, preferred_element_type=jnp.float32)
    low_rank = low_rank.reshape(inputs.shape[0], held_count, rank_size)
    keep_mask = slot_ids[:, None] == first_slot + jnp.arange(held_count, dtype=jnp.int32)[None, :]
    low_rank = jnp.where(keep_mask[:, :, None], low_rank, 0.0).astype(jnp.bfloat16)
    low_rank = low_rank.reshape(inputs.shape[0], held_count * rank_size)
    flat_up = up_store.reshape(held_count * rank_size, up_store.shape[2])
    return jnp.dot(low_rank, flat_up, preferred_element_type=jnp.float32)

def reference(tokens, norm_gain, routes, route_gates, lengths, request_adapter, adapter_slot, expert_gate, expert_up, expert_down, shared_gate, shared_up_weight, shared_down, adapter_down, adapter_up, head_weight):
    normed = apply_norm(tokens, norm_gain)
    bucket = DEVICES * CAP
    gate_values = route_gates.astype(jnp.float32)

    def one_expert(routed_output, inputs):
        number, gate_mat, up_mat, down_mat = inputs
        route_hits = routes == number
        chosen = jnp.any(route_hits, axis=1)
        weight = lax.optimization_barrier(jnp.sum(jnp.where(route_hits, gate_values, 0.0), axis=1))
        slot_place = (jnp.cumsum(chosen.astype(jnp.int32)) - 1).astype(jnp.int32)
        target = jnp.where(chosen, slot_place, bucket).astype(jnp.int32)
        row_order = jnp.zeros((bucket,), jnp.int32).at[target].set(jnp.arange(TOKENS, dtype=jnp.int32), mode='drop')
        outputs = feed_forward(normed[row_order], gate_mat, up_mat, down_mat).astype(jnp.bfloat16)
        fetched = outputs[jnp.clip(slot_place, 0, bucket - 1)].astype(jnp.float32)
        return (routed_output + weight[:, None] * fetched, None)
    routed_output, ignored = lax.scan(one_expert, jnp.zeros((TOKENS, D), jnp.float32), (jnp.arange(EXPERTS, dtype=jnp.int32), expert_gate, expert_up, expert_down))
    shared_sum = feed_forward(normed, shared_gate, shared_up_weight, shared_down)
    slot_ids = token_slots(jnp.arange(TOKENS, dtype=jnp.int32), lengths, request_adapter, adapter_slot)
    delta = adapter_delta(normed, slot_ids, adapter_down, adapter_up, 0)
    summed = routed_output + shared_sum + delta
    sublayer_out = summed.astype(jnp.bfloat16)
    request_ends = jnp.cumsum(lengths).astype(jnp.int32)
    last_rows = sublayer_out[request_ends - 1]
    last_values = last_rows.astype(jnp.float32)
    last_norm = jnp.sqrt(lax.optimization_barrier(jnp.sum(last_values * last_values, axis=1)))
    logits = jnp.dot(last_rows, head_weight, preferred_element_type=jnp.float32)
    block_logit = lax.optimization_barrier(jnp.max(logits.reshape(REQUESTS, N_DP, N_TENSOR, VOCAB // DEVICES), axis=(1, 3)))
    return (sublayer_out, last_norm, block_logit)
```

```python
import functools

import jax
import jax.numpy as jnp
from jax import lax
from jax.experimental import pallas as pl
from jax.experimental.pallas import tpu as pltpu
from jax.sharding import PartitionSpec as P

CAP = 32
HOPS = (0, 1, 3, 2)
PAD_ROWS = 32
F32 = jnp.float32
BF16 = jnp.bfloat16
MESH = pl.DeviceIdType.MESH


def body(
    lengths,
    request_adapter,
    adapter_slot,
    tokens,
    gain,
    meta_in,
    expert_gate,
    expert_up,
    expert_down,
    shared_gate,
    shared_up,
    shared_down,
    low_down,
    low_up,
    head,
    out,
    norm_out,
    logit_out,
    w_gate,
    w_up,
    w_down,
    w_sgate,
    w_sup,
    w_sdown,
    w_ldown,
    w_lup,
    w_head,
    first_rows,
    peer_rows,
    meta,
    picked,
    arrived,
    results,
    returned,
    mixing,
    hidden,
    part_send,
    part_recv,
    shared_send,
    shared_recv,
    total,
    slot_grid,
    last_mine,
    last_core,
    last_sum,
    last_recv,
    last_full,
    top_mine,
    top_recv,
    load_sem,
    meta_send_sem,
    meta_recv_sem,
    first_send_sem,
    first_recv_sem,
    peer_send_sem,
    peer_recv_sem,
    pick_send_sem,
    pick_recv_sem,
    ret_send_sem,
    ret_recv_sem,
    part_send_sem,
    part_recv_sem,
    shared_send_sem,
    shared_recv_sem,
    core_send_sem,
    core_recv_sem,
    last_send_sem,
    last_recv_sem,
    top_send_sem,
    top_recv_sem,
):
    width = tokens.shape[1]
    rows = tokens.shape[0]
    d = lax.axis_index("dp")
    t = lax.axis_index("tensor")
    y = t // 8
    z = (t // 2) % 4
    c = t % 2
    one = c == 1

    def at(ty, tz, tc):
        return (d, ty * 8 + tz * 2 + tc)

    def along_first(k):
        return at(
            jnp.where(one, y, (y + k) % 4),
            jnp.where(one, (z + k) % 4, z),
            c,
        )

    def along_x(k):
        return ((d + k) % 4, t)

    def expert_of(j):
        return jnp.where(one, (j // 2) * 8 + z * 2 + j % 2, y * 8 + j)

    own_j = jnp.where(one, y * 2 + 1, z * 2)
    own_q = jnp.where(one, 4 + y, z)

    def relay_of(q):
        return jnp.where(q < 4, y * 8 + q * 2, (q - 4) * 8 + z * 2 + 1)

    loads = []
    for i, (src, dst) in enumerate(
        (
            (shared_gate, w_sgate),
            (shared_up, w_sup),
            (low_down, w_ldown),
            (shared_down, w_sdown),
            (low_up, w_lup),
            (expert_gate.at[0], w_gate),
            (expert_up.at[0], w_up),
            (expert_down.at[0], w_down),
            (head, w_head),
        )
    ):
        loads.append(pltpu.make_async_copy(src, dst, load_sem.at[i]))
    for load in loads:
        load.start()

    barrier = pltpu.get_barrier_semaphore()
    greeted = [at(y, z, 1 - c)]
    for k in (1, 2, 3):
        for o in (0, 1):
            greeted.append(at(y, (z + k) % 4, o))
            greeted.append(at((y + k) % 4, z, o))
        greeted.append(along_x(k))
    for target in greeted:
        pl.semaphore_signal(barrier, inc=1, device_id=target, device_id_type=MESH)

    values = tokens[...].astype(F32)
    scaled = lax.rsqrt(jnp.mean(values * values, axis=-1, keepdims=True) + 1e-06)
    normed = (values * scaled * gain[...].astype(F32)).astype(BF16)
    first_rows[0] = normed
    peer_rows[0] = normed
    meta[0] = meta_in[...]

    lane = lax.broadcasted_iota(jnp.int32, (8, rows), 1)
    row = lax.broadcasted_iota(jnp.int32, (8, rows), 0)
    hop = jnp.where(row == 2, 3, jnp.where(row == 3, 2, row))
    place = (((d - hop + 8) % 4) * 32 + t) * rows + lane
    slots = jnp.zeros((8, rows), jnp.int32)
    pick_at = lax.broadcasted_iota(jnp.int32, (PAD_ROWS, rows), 0)
    own_place = (d * 32 + t) * rows + lax.broadcasted_iota(jnp.int32, (PAD_ROWS, rows), 1)
    last_pick = jnp.zeros((PAD_ROWS, rows), F32)
    start = jnp.int32(0)
    for r in range(lengths.shape[0]):
        slot = adapter_slot[request_adapter[r]]
        slots = jnp.where(place >= start, slot, slots)
        start = start + lengths[r]
        last_pick = jnp.where((pick_at == r) & (own_place == start - 1), 1.0, last_pick)
    slots = slots.astype(F32)
    for p in range(4):
        slot_grid[p] = jnp.transpose(jnp.broadcast_to(slots[p : p + 1], (rows, rows)))

    pl.semaphore_wait(barrier, len(greeted))

    def meta_copy(p):
        return pltpu.make_async_remote_copy(
            src_ref=meta.at[0],
            dst_ref=meta.at[p],
            send_sem=meta_send_sem.at[p],
            recv_sem=meta_recv_sem.at[p],
            device_id=along_first(HOPS[p]),
            device_id_type=MESH,
        )

    def first_copy(p):
        return pltpu.make_async_remote_copy(
            src_ref=first_rows.at[0],
            dst_ref=first_rows.at[p],
            send_sem=first_send_sem.at[p],
            recv_sem=first_recv_sem.at[p],
            device_id=along_first(HOPS[p]),
            device_id_type=MESH,
        )

    def peer_copy(p):
        return pltpu.make_async_remote_copy(
            src_ref=peer_rows.at[0],
            dst_ref=peer_rows.at[p],
            send_sem=peer_send_sem.at[p],
            recv_sem=peer_recv_sem.at[p],
            device_id=along_x(HOPS[p]),
            device_id_type=MESH,
        )

    for p in (1, 2, 3):
        meta_copy(p).start()
        first_copy(p).start()
    for p in (1, 2, 3):
        peer_copy(p).start()

    def pick_copy(p, j):
        return pltpu.make_async_remote_copy(
            src_ref=picked.at[p, j],
            dst_ref=arrived.at[p, own_q],
            send_sem=pick_send_sem.at[p, j],
            recv_sem=pick_recv_sem.at[p, own_q],
            device_id=(d, expert_of(j)),
            device_id_type=MESH,
        )

    def pick_wait(p, q):
        return pltpu.make_async_remote_copy(
            src_ref=picked.at[p, own_j],
            dst_ref=arrived.at[p, q],
            send_sem=pick_send_sem.at[p, own_j],
            recv_sem=pick_recv_sem.at[p, q],
            device_id=(d, relay_of(q)),
            device_id_type=MESH,
        )

    def own_at(q):
        return jnp.where(q < 4, z * 2 + c, y * 2 + c)

    def ret_copy(p, q):
        return pltpu.make_async_remote_copy(
            src_ref=results.at[p, q],
            dst_ref=returned.at[p, own_at(q)],
            send_sem=ret_send_sem.at[p, q],
            recv_sem=ret_recv_sem.at[p, own_at(q)],
            device_id=(d, relay_of(q)),
            device_id_type=MESH,
        )

    def ret_wait(p, j):
        return pltpu.make_async_remote_copy(
            src_ref=results.at[p, own_q],
            dst_ref=returned.at[p, j],
            send_sem=ret_send_sem.at[p, own_q],
            recv_sem=ret_recv_sem.at[p, j],
            device_id=(d, expert_of(j)),
            device_id_type=MESH,
        )

    def other_j(r):
        near = ((1, 0), (3, 0), (1, 1), (3, 1), (2, 0), (2, 1), (0, 1))[r]
        return ((own_j // 2 + near[0]) % 4) * 2 + (c + near[1]) % 2

    def other_q(r):
        return (own_q + r + 1) % 8

    tri_a = lax.broadcasted_iota(jnp.int32, (rows, rows), 0)
    tri_b = lax.broadcasted_iota(jnp.int32, (rows, rows), 1)
    upper = jnp.where(tri_a <= tri_b, 1.0, 0.0).astype(F32)
    index_j = lax.broadcasted_iota(jnp.int32, (8, rows), 0)
    wanted = expert_of(index_j).astype(F32)
    slot_index = lax.broadcasted_iota(jnp.int32, (8, CAP, rows), 1).astype(F32)

    def select(p):
        table = meta[p]
        chosen = jnp.zeros((8, rows), F32)
        weight = jnp.zeros((8, rows), F32)
        for k in range(6):
            same = table[k : k + 1, :] == wanted
            chosen = jnp.where(same, 1.0, chosen)
            weight = jnp.where(same, table[8 + k : 9 + k, :], weight)
        count = jnp.dot(chosen, upper, preferred_element_type=F32)
        slot_of = jnp.where(chosen > 0.5, count - 1.0, -1.0)
        hit = jnp.broadcast_to(slot_of[:, None, :], (8, CAP, rows)) == slot_index
        pick = jnp.where(hit, 1.0, 0.0).reshape(8 * CAP, rows).astype(BF16)
        mix = jnp.where(hit, jnp.broadcast_to(weight[:, None, :], (8, CAP, rows)), 0.0)
        mixing[p] = jnp.transpose(mix.reshape(8 * CAP, rows)).astype(BF16)

        def columns(n, carry):
            cols = pl.ds(pl.multiple_of(n * 512, 512), 512)
            got = jnp.dot(pick, first_rows[p, :, cols], preferred_element_type=F32)
            picked[p, :, :, cols] = got.astype(BF16).reshape(8, CAP, 512)
            return carry

        lax.fori_loop(0, width // 512, columns, 0)
        arrived[p, own_q] = picked[p, own_j]
        for r in range(7):
            pick_copy(p, other_j(r)).start()

    def shared(b):
        at_b = pl.ds(b * 2, 2)
        x = peer_rows[at_b].reshape(2 * rows, width)
        gate_part = jnp.dot(x, w_sgate[...], preferred_element_type=F32)
        up_part = jnp.dot(x, w_sup[...], preferred_element_type=F32)
        inner = (gate_part / (1.0 + jnp.exp(-gate_part)) * up_part).astype(BF16)
        low = jnp.dot(x, w_ldown[...], preferred_element_type=F32)
        lanes = lax.broadcasted_iota(jnp.int32, low.shape, 1) // 16 + d * 8
        keep = slot_grid[at_b].reshape(2 * rows, rows) == lanes.astype(F32)
        low = jnp.where(keep, low, 0.0).astype(BF16)

        def columns(n, carry):
            cols = pl.ds(pl.multiple_of(n * 512, 512), 512)
            part = jnp.dot(inner, w_sdown[:, cols], preferred_element_type=F32)
            part = part + jnp.dot(low, w_lup[:, cols], preferred_element_type=F32)
            shared_send[at_b, :, cols] = part.astype(BF16).reshape(2, rows, 512)

            @pl.when(b == 0)
            def _():
                total[:, cols] = part[:rows]

            return carry

        lax.fori_loop(0, width // 512, columns, 0)

    def shared_copy(p):
        return pltpu.make_async_remote_copy(
            src_ref=shared_send.at[p],
            dst_ref=shared_recv.at[p],
            send_sem=shared_send_sem.at[p],
            recv_sem=shared_recv_sem.at[p],
            device_id=along_x(4 - HOPS[p]),
            device_id_type=MESH,
        )

    def part_copy(p, hop):
        return pltpu.make_async_remote_copy(
            src_ref=part_send.at[p],
            dst_ref=part_recv.at[p],
            send_sem=part_send_sem.at[p],
            recv_sem=part_recv_sem.at[p],
            device_id=along_first(4 - hop),
            device_id_type=MESH,
        )

    inner_width = w_gate.shape[1]
    wide = inner_width // 256

    def gated(p, cols):
        x = arrived[p].reshape(8 * CAP, width)
        gate_part = jnp.dot(x, w_gate[:, cols], preferred_element_type=F32)
        up_part = jnp.dot(x, w_up[:, cols], preferred_element_type=F32)
        act = gate_part / (1.0 + jnp.exp(-gate_part)) * up_part
        hidden[:, cols] = act.astype(BF16)

    def expert(p):
        for r in range(7):
            pick_wait(p, other_q(r)).wait_recv()

        def columns(n, carry):
            gated(p, pl.ds(pl.multiple_of(n * 256, 256), 256))
            return carry

        lax.fori_loop(0, wide, columns, 0)
        if inner_width > wide * 256:
            gated(p, pl.ds(wide * 256, inner_width - wide * 256))

        def down(n, carry):
            cols = pl.ds(pl.multiple_of(n * 512, 512), 512)
            got = jnp.dot(hidden[...], w_down[:, cols], preferred_element_type=F32)
            results[p, :, :, cols] = got.astype(BF16).reshape(8, CAP, 512)
            return carry

        lax.fori_loop(0, width // 512, down, 0)
        returned[p, own_j] = results[p, own_q]
        for r in range(7):
            ret_copy(p, other_q(r)).start()

    def combine(p, own):
        for r in range(7):
            ret_wait(p, other_j(r)).wait_recv()

        def columns(n, carry):
            cols = pl.ds(pl.multiple_of(n * 512, 512), 512)
            got = jnp.dot(
                mixing[p],
                returned[p, :, :, cols].reshape(8 * CAP, 512),
                preferred_element_type=F32,
            )
            if own:
                total[:, cols] += got
            else:
                part_send[p, :, cols] = got.astype(BF16)
            return carry

        lax.fori_loop(0, width // 512, columns, 0)

    def select_step(p, carry):
        @pl.when(p > 0)
        def _():
            pltpu.make_async_remote_copy(
                src_ref=meta.at[0],
                dst_ref=meta.at[p],
                send_sem=meta_send_sem.at[p],
                recv_sem=meta_recv_sem.at[p],
                device_id=along_first(1),
                device_id_type=MESH,
            ).wait_recv()
            pltpu.make_async_remote_copy(
                src_ref=first_rows.at[0],
                dst_ref=first_rows.at[p],
                send_sem=first_send_sem.at[p],
                recv_sem=first_recv_sem.at[p],
                device_id=along_first(1),
                device_id_type=MESH,
            ).wait_recv()

        select(p)
        return carry

    lax.fori_loop(0, 4, select_step, 0)

    for load in loads[:5]:
        load.wait()
    peer_copy(1).wait_recv()

    def shared_step(b, carry):
        @pl.when(b == 1)
        def _():
            peer_copy(2).wait_recv()
            peer_copy(3).wait_recv()

        shared(b)
        return carry

    for load in loads[5:8]:
        load.wait()

    def expert_step(p, carry):
        expert(p)

        @pl.when(p < 2)
        def _():
            shared_step(p, 0)

            @pl.when(p == 0)
            def _():
                shared_copy(1).start()

            @pl.when(p == 1)
            def _():
                shared_copy(2).start()
                shared_copy(3).start()

        return carry

    lax.fori_loop(0, 4, expert_step, 0)
    combine(0, True)

    def combine_step(p, carry):
        combine(p, False)
        part_copy(p, jnp.where(p == 2, 3, jnp.where(p == 3, 2, p))).start()
        return carry

    lax.fori_loop(1, 4, combine_step, 0)

    for p in (1, 2, 3):
        shared_copy(p).wait_recv()
    for p in (1, 2, 3):
        part_copy(p, HOPS[p]).wait_recv()

    def finish(n, carry):
        cols = pl.ds(pl.multiple_of(n * 512, 512), 512)
        value = total[:, cols]
        for p in (1, 2, 3):
            value = value + shared_recv[p, :, cols].astype(F32)
            value = value + part_recv[p, :, cols].astype(F32)
        out[:, cols] = value.astype(BF16)
        return carry

    lax.fori_loop(0, width // 512, finish, 0)

    half = width // 2
    pick_last = last_pick.astype(BF16)
    for h in (0, 1):
        mine = jnp.dot(pick_last, out[:, h * half : (h + 1) * half], preferred_element_type=F32)
        last_mine[h] = mine.astype(BF16)

    def core_copy(i, src, dst):
        return pltpu.make_async_remote_copy(
            src_ref=src,
            dst_ref=dst,
            send_sem=core_send_sem.at[i],
            recv_sem=core_recv_sem.at[i],
            device_id=at(y, z, 1 - c),
            device_id_type=MESH,
        )

    swap = core_copy(0, last_mine.at[1 - c], last_core)
    swap.start()
    swap.wait_recv()
    last_sum[0] = (last_mine[c].astype(F32) + last_core[...].astype(F32)).astype(BF16)
    stage_copies = []
    for a in range(3):
        copies = []
        for k in (1, 3, 2):
            target = (at(y, (z + k) % 4, c), at((y + k) % 4, z, c), along_x(k))[a]
            copies.append(
                pltpu.make_async_remote_copy(
                    src_ref=last_sum.at[a],
                    dst_ref=last_recv.at[a, k],
                    send_sem=last_send_sem.at[a, k],
                    recv_sem=last_recv_sem.at[a, k],
                    device_id=target,
                    device_id_type=MESH,
                )
            )
        for copy in copies:
            copy.start()
        for copy in copies:
            copy.wait_recv()
        value = last_sum[a].astype(F32)
        for k in (1, 2, 3):
            value = value + last_recv[a, k].astype(F32)
        last_sum[a + 1] = value.astype(BF16)
        stage_copies += copies
    last_full[c] = last_sum[3]
    spread = core_copy(1, last_sum.at[3], last_full.at[c])
    spread.start()
    loads[8].wait()
    spread.wait_recv()

    square = jnp.zeros((PAD_ROWS, 1), F32)
    logits = jnp.zeros((PAD_ROWS, w_head.shape[1]), F32)
    for h in (0, 1):
        value = last_full[h]
        wide_value = value.astype(F32)
        square = square + jnp.sum(wide_value * wide_value, axis=1, keepdims=True)
        logits = logits + jnp.dot(
            value, w_head[h * half : (h + 1) * half, :], preferred_element_type=F32
        )
    norm_out[...] = jnp.sqrt(square)[: norm_out.shape[0]]
    best = jnp.max(logits, axis=1, keepdims=True)
    top_mine[...] = jnp.broadcast_to(best, top_mine.shape)
    top_copies = []
    for k in (1, 3, 2):
        top_copies.append(
            pltpu.make_async_remote_copy(
                src_ref=top_mine,
                dst_ref=top_recv.at[k],
                send_sem=top_send_sem.at[k],
                recv_sem=top_recv_sem.at[k],
                device_id=along_x(k),
                device_id_type=MESH,
            )
        )
    for copy in top_copies:
        copy.start()
    for copy in top_copies:
        copy.wait_recv()
    best = top_mine[...]
    for k in (1, 2, 3):
        best = jnp.maximum(best, top_recv[k])
    logit_out[...] = best[: logit_out.shape[0], :1]

    for p in (1, 2, 3):
        meta_copy(p).wait_send()
        first_copy(p).wait_send()
        peer_copy(p).wait_send()
        shared_copy(p).wait_send()
        part_copy(p, HOPS[p]).wait_send()

    def drain(p, carry):
        for r in range(7):
            pick_copy(p, other_j(r)).wait_send()
            ret_copy(p, other_q(r)).wait_send()
        return carry

    lax.fori_loop(0, 4, drain, 0)
    swap.wait_send()
    spread.wait_send()
    for copy in stage_copies + top_copies:
        copy.wait_send()


def local(
    tokens,
    norm_gain,
    routes,
    route_gates,
    lengths,
    request_adapter,
    adapter_slot,
    expert_gate,
    expert_up,
    expert_down,
    shared_gate,
    shared_up_weight,
    shared_down,
    adapter_down,
    adapter_up,
    head_weight,
):
    rows, width = tokens.shape
    inner_width = expert_gate.shape[2]
    shared_width = shared_gate.shape[1]
    held, _, rank = adapter_down.shape
    columns = head_weight.shape[1]
    requests = lengths.shape[0]
    meta = jnp.concatenate(
        [
            jnp.pad(routes.astype(F32).T, ((0, 2), (0, 0))),
            jnp.pad(route_gates.astype(F32).T, ((0, 2), (0, 0))),
        ],
        axis=0,
    )
    low_down = jnp.transpose(adapter_down, (1, 0, 2)).reshape(width, held * rank)
    low_up = adapter_up.reshape(held * rank, width)
    vmem = pl.BlockSpec(memory_space=pltpu.VMEM)
    smem = pl.BlockSpec(memory_space=pltpu.SMEM)
    anywhere = pl.BlockSpec(memory_space=pl.ANY)
    dma = pltpu.SemaphoreType.DMA
    half = width // 2
    sublayer, last_norm, block_logit = pl.pallas_call(
        body,
        out_shape=(
            jax.ShapeDtypeStruct((rows, width), BF16),
            jax.ShapeDtypeStruct((requests, 1), F32),
            jax.ShapeDtypeStruct((requests, 1), F32),
        ),
        in_specs=[smem] * 3 + [vmem] * 3 + [anywhere] * 9,
        out_specs=(vmem, vmem, vmem),
        scratch_shapes=[
            pltpu.VMEM((width, inner_width), BF16),
            pltpu.VMEM((width, inner_width), BF16),
            pltpu.VMEM((inner_width, width), BF16),
            pltpu.VMEM((width, shared_width), BF16),
            pltpu.VMEM((width, shared_width), BF16),
            pltpu.VMEM((shared_width, width), BF16),
            pltpu.VMEM((width, held * rank), BF16),
            pltpu.VMEM((held * rank, width), BF16),
            pltpu.VMEM((width, columns), BF16),
            pltpu.VMEM((4, rows, width), BF16),
            pltpu.VMEM((4, rows, width), BF16),
            pltpu.VMEM((4, 16, rows), F32),
            pltpu.VMEM((4, 8, CAP, width), BF16),
            pltpu.VMEM((4, 8, CAP, width), BF16),
            pltpu.VMEM((4, 8, CAP, width), BF16),
            pltpu.VMEM((4, 8, CAP, width), BF16),
            pltpu.VMEM((4, rows, 8 * CAP), BF16),
            pltpu.VMEM((8 * CAP, inner_width), BF16),
            pltpu.VMEM((4, rows, width), BF16),
            pltpu.VMEM((4, rows, width), BF16),
            pltpu.VMEM((4, rows, width), BF16),
            pltpu.VMEM((4, rows, width), BF16),
            pltpu.VMEM((rows, width), F32),
            pltpu.VMEM((4, rows, rows), F32),
            pltpu.VMEM((2, PAD_ROWS, half), BF16),
            pltpu.VMEM((PAD_ROWS, half), BF16),
            pltpu.VMEM((4, PAD_ROWS, half), BF16),
            pltpu.VMEM((3, 4, PAD_ROWS, half), BF16),
            pltpu.VMEM((2, PAD_ROWS, half), BF16),
            pltpu.VMEM((PAD_ROWS, 128), F32),
            pltpu.VMEM((4, PAD_ROWS, 128), F32),
            dma((9,)),
            dma((4,)),
            dma((4,)),
            dma((4,)),
            dma((4,)),
            dma((4,)),
            dma((4,)),
            dma((4, 8)),
            dma((4, 8)),
            dma((4, 8)),
            dma((4, 8)),
            dma((4,)),
            dma((4,)),
            dma((4,)),
            dma((4,)),
            dma((2,)),
            dma((2,)),
            dma((3, 4)),
            dma((3, 4)),
            dma((4,)),
            dma((4,)),
        ],
        compiler_params=pltpu.CompilerParams(
            collective_id=0, has_side_effects=True, vmem_limit_bytes=63 << 20
        ),
        name="sublayer",
    )(
        lengths,
        request_adapter,
        adapter_slot,
        tokens,
        norm_gain.reshape(1, width),
        meta,
        expert_gate,
        expert_up,
        expert_down,
        shared_gate,
        shared_up_weight,
        shared_down,
        low_down,
        low_up,
        head_weight,
    )
    return (sublayer, last_norm.reshape(requests), block_logit)


def solution(mesh):
    placed = (
        P(("dp", "tensor"), None),
        P(),
        P(("dp", "tensor"), None),
        P(("dp", "tensor"), None),
        P(),
        P(),
        P(),
        P("tensor", None, None),
        P("tensor", None, None),
        P("tensor", None, None),
        P(None, "dp"),
        P(None, "dp"),
        P("dp", None),
        P("dp", None, None),
        P("dp", None, None),
        P(None, ("dp", "tensor")),
    )
    return jax.shard_map(
        local,
        mesh=mesh,
        in_specs=placed,
        out_specs=(P(("dp", "tensor"), None), P(), P(None, "tensor")),
        check_vma=False,
    )
```

```python
import functools

import jax
import jax.numpy as jnp
from jax import lax
from jax.experimental import pallas as pl
from jax.experimental.pallas import tpu as pltpu
from jax.sharding import PartitionSpec as P

CAP = 32
HOPS = (0, 1, 3, 2)
PAD_ROWS = 32
F32 = jnp.float32
BF16 = jnp.bfloat16
MESH = pl.DeviceIdType.MESH


def dot_rows(a, b):
    return lax.dot_general(a, b, (((1,), (1,)), ((), ())), preferred_element_type=F32)


def body(
    lengths,
    request_adapter,
    adapter_slot,
    tokens,
    gain,
    routes_in,
    gates_in,
    expert_gate,
    expert_up,
    expert_down,
    shared_gate,
    shared_up,
    shared_down,
    low_down,
    low_up,
    head,
    out,
    norm_out,
    logit_out,
    w_gate,
    w_up,
    w_down,
    w_sgate,
    w_sup,
    w_sdown,
    w_ldown,
    w_lup,
    w_head,
    first_rows,
    peer_rows,
    meta,
    picked,
    arrived,
    results,
    returned,
    mixing,
    hidden,
    part_send,
    part_recv,
    shared_send,
    shared_recv,
    total,
    slot_grid,
    last_mine,
    last_core,
    last_sum,
    last_recv,
    last_full,
    top_mine,
    top_recv,
    load_sem,
    meta_send_sem,
    meta_recv_sem,
    first_send_sem,
    first_recv_sem,
    peer_send_sem,
    peer_recv_sem,
    pick_send_sem,
    pick_recv_sem,
    ret_send_sem,
    ret_recv_sem,
    part_send_sem,
    part_recv_sem,
    shared_send_sem,
    shared_recv_sem,
    core_send_sem,
    core_recv_sem,
    last_send_sem,
    last_recv_sem,
    top_send_sem,
    top_recv_sem,
):
    width = tokens.shape[1]
    rows = tokens.shape[0]
    d = lax.axis_index("dp")
    t = lax.axis_index("tensor")
    y = t // 8
    z = (t // 2) % 4
    c = t % 2
    one = c == 1

    def at(ty, tz, tc):
        return (d, ty * 8 + tz * 2 + tc)

    def along_first(k):
        return at(
            jnp.where(one, y, (y + k) % 4),
            jnp.where(one, (z + k) % 4, z),
            c,
        )

    def along_x(k):
        return ((d + k) % 4, t)

    def expert_of(j):
        return jnp.where(one, (j // 2) * 8 + z * 2 + j % 2, y * 8 + j)

    own_j = jnp.where(one, y * 2 + 1, z * 2)
    own_q = jnp.where(one, 4 + y, z)

    def relay_of(q):
        return jnp.where(q < 4, y * 8 + q * 2, (q - 4) * 8 + z * 2 + 1)

    loads = []
    for i, (src, dst) in enumerate(
        (
            (shared_gate, w_sgate),
            (shared_up, w_sup),
            (low_down, w_ldown),
            (shared_down, w_sdown),
            (low_up, w_lup),
            (expert_gate.at[0], w_gate),
            (expert_up.at[0], w_up),
            (expert_down.at[0], w_down),
            (head, w_head),
        )
    ):
        loads.append(pltpu.make_async_copy(src, dst, load_sem.at[i]))
    for load in loads:
        load.start()

    barrier = pltpu.get_barrier_semaphore()
    greeted = [at(y, z, 1 - c)]
    for k in (1, 2, 3):
        for o in (0, 1):
            greeted.append(at(y, (z + k) % 4, o))
            greeted.append(at((y + k) % 4, z, o))
        greeted.append(along_x(k))
    for target in greeted:
        pl.semaphore_signal(barrier, inc=1, device_id=target, device_id_type=MESH)

    values = tokens[...].astype(F32)
    scaled = lax.rsqrt(jnp.mean(values * values, axis=-1, keepdims=True) + 1e-06)
    gains = gain[...].astype(F32).reshape(1, width)
    normed = (values * scaled * gains).astype(BF16)
    first_rows[0] = normed
    peer_rows[0] = normed
    meta[0] = jnp.zeros_like(meta[0])
    meta[0, 0:6] = routes_in[...].astype(F32)
    meta[0, 8:14] = gates_in[...].astype(F32)

    lane = lax.broadcasted_iota(jnp.int32, (8, rows), 1)
    row = lax.broadcasted_iota(jnp.int32, (8, rows), 0)
    hop = jnp.where(row == 2, 3, jnp.where(row == 3, 2, row))
    place = (((d - hop + 8) % 4) * 32 + t) * rows + lane
    slots = jnp.zeros((8, rows), jnp.int32)
    pick_at = lax.broadcasted_iota(jnp.int32, (PAD_ROWS, rows), 0)
    own_place = (d * 32 + t) * rows + lax.broadcasted_iota(jnp.int32, (PAD_ROWS, rows), 1)
    last_pick = jnp.zeros((PAD_ROWS, rows), F32)
    start = jnp.int32(0)
    for r in range(lengths.shape[0]):
        slot = adapter_slot[request_adapter[r]]
        slots = jnp.where(place >= start, slot, slots)
        start = start + lengths[r]
        last_pick = jnp.where((pick_at == r) & (own_place == start - 1), 1.0, last_pick)
    slots = slots.astype(F32)
    for p in range(4):
        slot_grid[p] = jnp.transpose(jnp.broadcast_to(slots[p : p + 1], (rows, rows)))

    pl.semaphore_wait(barrier, len(greeted))

    def meta_copy(p):
        return pltpu.make_async_remote_copy(
            src_ref=meta.at[0],
            dst_ref=meta.at[p],
            send_sem=meta_send_sem.at[p],
            recv_sem=meta_recv_sem.at[p],
            device_id=along_first(HOPS[p]),
            device_id_type=MESH,
        )

    def first_copy(p):
        return pltpu.make_async_remote_copy(
            src_ref=first_rows.at[0],
            dst_ref=first_rows.at[p],
            send_sem=first_send_sem.at[p],
            recv_sem=first_recv_sem.at[p],
            device_id=along_first(HOPS[p]),
            device_id_type=MESH,
        )

    def peer_copy(p):
        return pltpu.make_async_remote_copy(
            src_ref=peer_rows.at[0],
            dst_ref=peer_rows.at[p],
            send_sem=peer_send_sem.at[p],
            recv_sem=peer_recv_sem.at[p],
            device_id=along_x(HOPS[p]),
            device_id_type=MESH,
        )

    for p in (1, 2, 3):
        meta_copy(p).start()
        first_copy(p).start()
    for p in (1, 2, 3):
        peer_copy(p).start()

    def pick_copy(p, j):
        return pltpu.make_async_remote_copy(
            src_ref=picked.at[p, j],
            dst_ref=arrived.at[p, own_q],
            send_sem=pick_send_sem.at[p, j],
            recv_sem=pick_recv_sem.at[p, own_q],
            device_id=(d, expert_of(j)),
            device_id_type=MESH,
        )

    def pick_wait(p, q):
        return pltpu.make_async_remote_copy(
            src_ref=picked.at[p, own_j],
            dst_ref=arrived.at[p, q],
            send_sem=pick_send_sem.at[p, own_j],
            recv_sem=pick_recv_sem.at[p, q],
            device_id=(d, relay_of(q)),
            device_id_type=MESH,
        )

    def own_at(q):
        return jnp.where(q < 4, z * 2 + c, y * 2 + c)

    def ret_copy(p, q):
        return pltpu.make_async_remote_copy(
            src_ref=results.at[p, q],
            dst_ref=returned.at[p, own_at(q)],
            send_sem=ret_send_sem.at[p, q],
            recv_sem=ret_recv_sem.at[p, own_at(q)],
            device_id=(d, relay_of(q)),
            device_id_type=MESH,
        )

    def ret_wait(p, j):
        return pltpu.make_async_remote_copy(
            src_ref=results.at[p, own_q],
            dst_ref=returned.at[p, j],
            send_sem=ret_send_sem.at[p, own_q],
            recv_sem=ret_recv_sem.at[p, j],
            device_id=(d, expert_of(j)),
            device_id_type=MESH,
        )

    def other_j(r):
        near = ((1, 0), (3, 0), (1, 1), (3, 1), (2, 0), (2, 1), (0, 1))[r]
        return ((own_j // 2 + near[0]) % 4) * 2 + (c + near[1]) % 2

    def other_q(r):
        return (own_q + r + 1) % 8

    tri_a = lax.broadcasted_iota(jnp.int32, (rows, rows), 0)
    tri_b = lax.broadcasted_iota(jnp.int32, (rows, rows), 1)
    upper = jnp.where(tri_a <= tri_b, 1.0, 0.0).astype(F32)
    index_j = lax.broadcasted_iota(jnp.int32, (8, rows), 0)
    wanted = expert_of(index_j).astype(F32)
    slot_index = lax.broadcasted_iota(jnp.int32, (8, CAP, rows), 1).astype(F32)

    def select(p):
        table = meta[p]
        chosen = jnp.zeros((8, rows), F32)
        weight = jnp.zeros((8, rows), F32)
        for k in range(6):
            same = table[k : k + 1, :] == wanted
            chosen = jnp.where(same, 1.0, chosen)
            weight = jnp.where(same, table[8 + k : 9 + k, :], weight)
        count = jnp.dot(chosen, upper, preferred_element_type=F32)
        slot_of = jnp.where(chosen > 0.5, count - 1.0, -1.0)
        hit = jnp.broadcast_to(slot_of[:, None, :], (8, CAP, rows)) == slot_index
        pick = jnp.where(hit, 1.0, 0.0).reshape(8 * CAP, rows).astype(BF16)
        mix = jnp.where(hit, jnp.broadcast_to(weight[:, None, :], (8, CAP, rows)), 0.0)
        mixing[p] = jnp.transpose(mix.reshape(8 * CAP, rows)).astype(BF16)

        def columns(n, carry):
            cols = pl.ds(pl.multiple_of(n * 512, 512), 512)
            got = jnp.dot(pick, first_rows[p, :, cols], preferred_element_type=F32)
            picked[p, :, :, cols] = got.astype(BF16).reshape(8, CAP, 512)
            return carry

        lax.fori_loop(0, width // 512, columns, 0)
        arrived[p, own_q] = picked[p, own_j]
        for r in range(7):
            pick_copy(p, other_j(r)).start()

    def shared(b):
        at_b = pl.ds(b * 2, 2)
        x = peer_rows[at_b].reshape(2 * rows, width)
        gate_part = dot_rows(x, w_sgate[...])
        up_part = dot_rows(x, w_sup[...])
        inner = (gate_part / (1.0 + jnp.exp(-gate_part)) * up_part).astype(BF16)
        low = dot_rows(x, w_ldown[...])
        lanes = lax.broadcasted_iota(jnp.int32, low.shape, 1) // 16 + d * 8
        keep = slot_grid[at_b].reshape(2 * rows, rows) == lanes.astype(F32)
        low = jnp.where(keep, low, 0.0).astype(BF16)

        def columns(n, carry):
            cols = pl.ds(pl.multiple_of(n * 512, 512), 512)
            part = jnp.dot(inner, w_sdown[:, cols], preferred_element_type=F32)
            part = part + jnp.dot(low, w_lup[:, cols], preferred_element_type=F32)
            shared_send[at_b, :, cols] = part.astype(BF16).reshape(2, rows, 512)

            @pl.when(b == 0)
            def _():
                total[:, cols] = part[:rows]

            return carry

        lax.fori_loop(0, width // 512, columns, 0)

    def shared_copy(p):
        return pltpu.make_async_remote_copy(
            src_ref=shared_send.at[p],
            dst_ref=shared_recv.at[p],
            send_sem=shared_send_sem.at[p],
            recv_sem=shared_recv_sem.at[p],
            device_id=along_x(4 - HOPS[p]),
            device_id_type=MESH,
        )

    def part_copy(p, hop):
        return pltpu.make_async_remote_copy(
            src_ref=part_send.at[p],
            dst_ref=part_recv.at[p],
            send_sem=part_send_sem.at[p],
            recv_sem=part_recv_sem.at[p],
            device_id=along_first(4 - hop),
            device_id_type=MESH,
        )

    inner_width = w_gate.shape[1]
    wide = inner_width // 256

    def gated(p, cols):
        x = arrived[p].reshape(8 * CAP, width)
        gate_part = jnp.dot(x, w_gate[:, cols], preferred_element_type=F32)
        up_part = jnp.dot(x, w_up[:, cols], preferred_element_type=F32)
        act = gate_part / (1.0 + jnp.exp(-gate_part)) * up_part
        hidden[:, cols] = act.astype(BF16)

    def expert(p):
        for r in range(7):
            pick_wait(p, other_q(r)).wait_recv()

        def columns(n, carry):
            gated(p, pl.ds(pl.multiple_of(n * 256, 256), 256))
            return carry

        lax.fori_loop(0, wide, columns, 0)
        if inner_width > wide * 256:
            gated(p, pl.ds(wide * 256, inner_width - wide * 256))

        def down(n, carry):
            cols = pl.ds(pl.multiple_of(n * 512, 512), 512)
            got = jnp.dot(hidden[...], w_down[:, cols], preferred_element_type=F32)
            results[p, :, :, cols] = got.astype(BF16).reshape(8, CAP, 512)
            return carry

        lax.fori_loop(0, width // 512, down, 0)
        returned[p, own_j] = results[p, own_q]
        for r in range(7):
            ret_copy(p, other_q(r)).start()

    def combine(p, own):
        for r in range(7):
            ret_wait(p, other_j(r)).wait_recv()

        def columns(n, carry):
            cols = pl.ds(pl.multiple_of(n * 512, 512), 512)
            got = jnp.dot(
                mixing[p],
                returned[p, :, :, cols].reshape(8 * CAP, 512),
                preferred_element_type=F32,
            )
            if own:
                total[:, cols] += got
            else:
                part_send[p, :, cols] = got.astype(BF16)
            return carry

        lax.fori_loop(0, width // 512, columns, 0)

    def select_step(p, carry):
        @pl.when(p > 0)
        def _():
            pltpu.make_async_remote_copy(
                src_ref=meta.at[0],
                dst_ref=meta.at[p],
                send_sem=meta_send_sem.at[p],
                recv_sem=meta_recv_sem.at[p],
                device_id=along_first(1),
                device_id_type=MESH,
            ).wait_recv()
            pltpu.make_async_remote_copy(
                src_ref=first_rows.at[0],
                dst_ref=first_rows.at[p],
                send_sem=first_send_sem.at[p],
                recv_sem=first_recv_sem.at[p],
                device_id=along_first(1),
                device_id_type=MESH,
            ).wait_recv()

        select(p)
        return carry

    lax.fori_loop(0, 4, select_step, 0)

    for load in loads[:5]:
        load.wait()
    peer_copy(1).wait_recv()

    def shared_step(b, carry):
        @pl.when(b == 1)
        def _():
            peer_copy(2).wait_recv()
            peer_copy(3).wait_recv()

        shared(b)
        return carry

    for load in loads[5:8]:
        load.wait()

    def expert_step(p, carry):
        expert(p)

        @pl.when(p < 2)
        def _():
            shared_step(p, 0)

            @pl.when(p == 0)
            def _():
                shared_copy(1).start()

            @pl.when(p == 1)
            def _():
                shared_copy(2).start()
                shared_copy(3).start()

        return carry

    lax.fori_loop(0, 4, expert_step, 0)
    combine(0, True)

    def combine_step(p, carry):
        combine(p, False)
        part_copy(p, jnp.where(p == 2, 3, jnp.where(p == 3, 2, p))).start()
        return carry

    lax.fori_loop(1, 4, combine_step, 0)

    for p in (1, 2, 3):
        shared_copy(p).wait_recv()
    for p in (1, 2, 3):
        part_copy(p, HOPS[p]).wait_recv()

    def finish(n, carry):
        cols = pl.ds(pl.multiple_of(n * 512, 512), 512)
        value = total[:, cols]
        for p in (1, 2, 3):
            value = value + shared_recv[p, :, cols].astype(F32)
            value = value + part_recv[p, :, cols].astype(F32)
        out[:, cols] = value.astype(BF16)
        return carry

    lax.fori_loop(0, width // 512, finish, 0)

    half = width // 2
    pick_last = last_pick.astype(BF16)
    for h in (0, 1):
        mine = jnp.dot(pick_last, out[:, h * half : (h + 1) * half], preferred_element_type=F32)
        last_mine[h] = mine.astype(BF16)

    def core_copy(i, src, dst):
        return pltpu.make_async_remote_copy(
            src_ref=src,
            dst_ref=dst,
            send_sem=core_send_sem.at[i],
            recv_sem=core_recv_sem.at[i],
            device_id=at(y, z, 1 - c),
            device_id_type=MESH,
        )

    swap = core_copy(0, last_mine.at[1 - c], last_core)
    swap.start()
    swap.wait_recv()
    last_sum[0] = (last_mine[c].astype(F32) + last_core[...].astype(F32)).astype(BF16)
    stage_copies = []
    third = half // 384 * 128
    groups = ((0, third), (third, third), (2 * third, half - 2 * third))
    for a in range(3):
        copies = []
        for k in (1, 3, 2):
            for g, (off, size) in enumerate(groups):
                targets = (at(y, (z + k) % 4, c), at((y + k) % 4, z, c), along_x(k))
                copies.append(
                    pltpu.make_async_remote_copy(
                        src_ref=last_sum.at[a, :, pl.ds(off, size)],
                        dst_ref=last_recv.at[a, k, :, pl.ds(off, size)],
                        send_sem=last_send_sem.at[a, g, k],
                        recv_sem=last_recv_sem.at[a, g, k],
                        device_id=targets[(a + g) % 3],
                        device_id_type=MESH,
                    )
                )
        for copy in copies:
            copy.start()
        for copy in copies:
            copy.wait_recv()
        value = last_sum[a].astype(F32)
        for k in (1, 2, 3):
            value = value + last_recv[a, k].astype(F32)
        last_sum[a + 1] = value.astype(BF16)
        stage_copies += copies
    last_full[c] = last_sum[3]
    spread = core_copy(1, last_sum.at[3], last_full.at[c])
    spread.start()
    loads[8].wait()
    spread.wait_recv()

    square = jnp.zeros((PAD_ROWS, 1), F32)
    logits = jnp.zeros((PAD_ROWS, w_head.shape[1]), F32)
    for h in (0, 1):
        value = last_full[h]
        wide_value = value.astype(F32)
        square = square + jnp.sum(wide_value * wide_value, axis=1, keepdims=True)
        logits = logits + jnp.dot(
            value, w_head[h * half : (h + 1) * half, :], preferred_element_type=F32
        )
    requests = norm_out.shape[0]
    norms = jnp.transpose(jnp.broadcast_to(jnp.sqrt(square), top_mine.shape))
    norm_out[...] = norms[:1, :requests].reshape(requests)
    best = jnp.max(logits, axis=1, keepdims=True)
    top_mine[...] = jnp.broadcast_to(best, top_mine.shape)
    top_copies = []
    for k in (1, 3, 2):
        top_copies.append(
            pltpu.make_async_remote_copy(
                src_ref=top_mine,
                dst_ref=top_recv.at[k],
                send_sem=top_send_sem.at[k],
                recv_sem=top_recv_sem.at[k],
                device_id=along_x(k),
                device_id_type=MESH,
            )
        )
    for copy in top_copies:
        copy.start()
    for copy in top_copies:
        copy.wait_recv()
    best = top_mine[...]
    for k in (1, 2, 3):
        best = jnp.maximum(best, top_recv[k])
    logit_out[...] = jnp.transpose(best)[:1, :requests]

    for p in (1, 2, 3):
        meta_copy(p).wait_send()
        first_copy(p).wait_send()
        peer_copy(p).wait_send()
        shared_copy(p).wait_send()
        part_copy(p, HOPS[p]).wait_send()

    def drain(p, carry):
        for r in range(7):
            pick_copy(p, other_j(r)).wait_send()
            ret_copy(p, other_q(r)).wait_send()
        return carry

    lax.fori_loop(0, 4, drain, 0)
    swap.wait_send()
    spread.wait_send()
    for copy in stage_copies + top_copies:
        copy.wait_send()


def local(
    tokens,
    norm_gain,
    routes,
    route_gates,
    lengths,
    request_adapter,
    adapter_slot,
    expert_gate,
    expert_up,
    expert_down,
    shared_gate,
    shared_up_weight,
    shared_down,
    adapter_down,
    adapter_up,
    head_weight,
):
    rows, width = tokens.shape
    inner_width = expert_gate.shape[2]
    shared_width = shared_gate.shape[1]
    held, _, rank = adapter_down.shape
    columns = head_weight.shape[1]
    requests = lengths.shape[0]
    low_down = jnp.transpose(adapter_down, (0, 2, 1)).reshape(held * rank, width)
    low_up = adapter_up.reshape(held * rank, width)
    vmem = pl.BlockSpec(memory_space=pltpu.VMEM)
    smem = pl.BlockSpec(memory_space=pltpu.SMEM)
    anywhere = pl.BlockSpec(memory_space=pl.ANY)
    dma = pltpu.SemaphoreType.DMA
    half = width // 2
    sublayer, last_norm, block_logit = pl.pallas_call(
        body,
        out_shape=(
            jax.ShapeDtypeStruct((rows, width), BF16),
            jax.ShapeDtypeStruct((requests,), F32),
            jax.ShapeDtypeStruct((1, requests), F32),
        ),
        in_specs=[smem] * 3 + [vmem] * 4 + [anywhere] * 9,
        out_specs=(vmem, vmem, vmem),
        scratch_shapes=[
            pltpu.VMEM((width, inner_width), BF16),
            pltpu.VMEM((width, inner_width), BF16),
            pltpu.VMEM((inner_width, width), BF16),
            pltpu.VMEM((shared_width, width), BF16),
            pltpu.VMEM((shared_width, width), BF16),
            pltpu.VMEM((shared_width, width), BF16),
            pltpu.VMEM((held * rank, width), BF16),
            pltpu.VMEM((held * rank, width), BF16),
            pltpu.VMEM((width, columns), BF16),
            pltpu.VMEM((4, rows, width), BF16),
            pltpu.VMEM((4, rows, width), BF16),
            pltpu.VMEM((4, 16, rows), F32),
            pltpu.VMEM((4, 8, CAP, width), BF16),
            pltpu.VMEM((4, 8, CAP, width), BF16),
            pltpu.VMEM((4, 8, CAP, width), BF16),
            pltpu.VMEM((4, 8, CAP, width), BF16),
            pltpu.VMEM((4, rows, 8 * CAP), BF16),
            pltpu.VMEM((8 * CAP, inner_width), BF16),
            pltpu.VMEM((4, rows, width), BF16),
            pltpu.VMEM((4, rows, width), BF16),
            pltpu.VMEM((4, rows, width), BF16),
            pltpu.VMEM((4, rows, width), BF16),
            pltpu.VMEM((rows, width), F32),
            pltpu.VMEM((4, rows, rows), F32),
            pltpu.VMEM((2, PAD_ROWS, half), BF16),
            pltpu.VMEM((PAD_ROWS, half), BF16),
            pltpu.VMEM((4, PAD_ROWS, half), BF16),
            pltpu.VMEM((3, 4, PAD_ROWS, half), BF16),
            pltpu.VMEM((2, PAD_ROWS, half), BF16),
            pltpu.VMEM((PAD_ROWS, 128), F32),
            pltpu.VMEM((4, PAD_ROWS, 128), F32),
            dma((9,)),
            dma((4,)),
            dma((4,)),
            dma((4,)),
            dma((4,)),
            dma((4,)),
            dma((4,)),
            dma((4, 8)),
            dma((4, 8)),
            dma((4, 8)),
            dma((4, 8)),
            dma((4,)),
            dma((4,)),
            dma((4,)),
            dma((4,)),
            dma((2,)),
            dma((2,)),
            dma((3, 3, 4)),
            dma((3, 3, 4)),
            dma((4,)),
            dma((4,)),
        ],
        compiler_params=pltpu.CompilerParams(
            collective_id=0, has_side_effects=True, vmem_limit_bytes=63 << 20
        ),
        name="sublayer",
    )(
        lengths,
        request_adapter,
        adapter_slot,
        tokens,
        norm_gain,
        routes.T,
        route_gates.T,
        expert_gate,
        expert_up,
        expert_down,
        shared_gate.T,
        shared_up_weight.T,
        shared_down,
        low_down,
        low_up,
        head_weight,
    )
    return (sublayer, last_norm, block_logit.T)


def solution(mesh):
    placed = (
        P(("dp", "tensor"), None),
        P(),
        P(("dp", "tensor"), None),
        P(("dp", "tensor"), None),
        P(),
        P(),
        P(),
        P("tensor", None, None),
        P("tensor", None, None),
        P("tensor", None, None),
        P(None, "dp"),
        P(None, "dp"),
        P("dp", None),
        P("dp", None, None),
        P("dp", None, None),
        P(None, ("dp", "tensor")),
    )
    return jax.shard_map(
        local,
        mesh=mesh,
        in_specs=placed,
        out_specs=(P(("dp", "tensor"), None), P(), P(None, "tensor")),
        check_vma=False,
    )
```

```python
import functools

import jax
import jax.numpy as jnp
from jax import lax
from jax.experimental import pallas as pl
from jax.experimental.pallas import tpu as pltpu
from jax.sharding import PartitionSpec as P

CAP = 32
HOPS = (0, 1, 3, 2)
PAD_ROWS = 32
F32 = jnp.float32
BF16 = jnp.bfloat16
MESH = pl.DeviceIdType.MESH


def dot_rows(a, b):
    return lax.dot_general(a, b, (((1,), (1,)), ((), ())), preferred_element_type=F32)


def body(
    lengths,
    request_adapter,
    adapter_slot,
    tokens,
    gain,
    routes_in,
    gates_in,
    expert_gate,
    expert_up,
    expert_down,
    shared_gate,
    shared_up,
    shared_down,
    low_down,
    low_up,
    head,
    out,
    norm_out,
    logit_out,
    w_gate,
    w_up,
    w_down,
    w_sgate,
    w_sup,
    w_sdown,
    w_ldown,
    w_lup,
    w_head,
    first_rows,
    peer_rows,
    meta,
    picked,
    arrived,
    results,
    returned,
    mixing,
    hidden,
    part_send,
    part_recv,
    shared_send,
    shared_recv,
    total,
    slot_grid,
    last_mine,
    last_core,
    last_sum,
    last_recv,
    last_full,
    top_mine,
    top_recv,
    load_sem,
    meta_send_sem,
    meta_recv_sem,
    first_send_sem,
    first_recv_sem,
    peer_send_sem,
    peer_recv_sem,
    pick_send_sem,
    pick_recv_sem,
    ret_send_sem,
    ret_recv_sem,
    part_send_sem,
    part_recv_sem,
    shared_send_sem,
    shared_recv_sem,
    core_send_sem,
    core_recv_sem,
    last_send_sem,
    last_recv_sem,
    top_send_sem,
    top_recv_sem,
):
    width = tokens.shape[1]
    rows = tokens.shape[0]
    d = lax.axis_index("dp")
    t = lax.axis_index("tensor")
    y = t // 8
    z = (t // 2) % 4
    c = t % 2
    one = c == 1

    def at(ty, tz, tc):
        return (d, ty * 8 + tz * 2 + tc)

    def along_first(k):
        return at(
            jnp.where(one, y, (y + k) % 4),
            jnp.where(one, (z + k) % 4, z),
            c,
        )

    def along_x(k):
        return ((d + k) % 4, t)

    def expert_of(j):
        return jnp.where(one, (j // 2) * 8 + z * 2 + j % 2, y * 8 + j)

    own_j = jnp.where(one, y * 2 + 1, z * 2)
    own_q = jnp.where(one, 4 + y, z)

    def relay_of(q):
        return jnp.where(q < 4, y * 8 + q * 2, (q - 4) * 8 + z * 2 + 1)

    loads = []
    for i, (src, dst) in enumerate(
        (
            (shared_gate, w_sgate),
            (shared_up, w_sup),
            (low_down, w_ldown),
            (shared_down, w_sdown),
            (low_up, w_lup),
            (expert_gate.at[0], w_gate),
            (expert_up.at[0], w_up),
            (expert_down.at[0], w_down),
            (head, w_head),
        )
    ):
        loads.append(pltpu.make_async_copy(src, dst, load_sem.at[i]))
    for load in loads:
        load.start()

    barrier = pltpu.get_barrier_semaphore()
    greeted = [at(y, z, 1 - c)]
    for k in (1, 2, 3):
        for o in (0, 1):
            greeted.append(at(y, (z + k) % 4, o))
            greeted.append(at((y + k) % 4, z, o))
        greeted.append(along_x(k))
    for target in greeted:
        pl.semaphore_signal(barrier, inc=1, device_id=target, device_id_type=MESH)

    values = tokens[...].astype(F32)
    scaled = lax.rsqrt(jnp.mean(values * values, axis=-1, keepdims=True) + 1e-06)
    gains = gain[...].astype(F32).reshape(1, width)
    normed = (values * scaled * gains).astype(BF16)
    first_rows[0] = normed
    peer_rows[0] = normed
    meta[0] = jnp.zeros_like(meta[0])
    meta[0, 0:6] = routes_in[...].astype(F32)
    meta[0, 8:14] = gates_in[...].astype(F32)

    lane = lax.broadcasted_iota(jnp.int32, (8, rows), 1)
    row = lax.broadcasted_iota(jnp.int32, (8, rows), 0)
    hop = jnp.where(row == 2, 3, jnp.where(row == 3, 2, row))
    place = (((d - hop + 8) % 4) * 32 + t) * rows + lane
    slots = jnp.zeros((8, rows), jnp.int32)
    pick_at = lax.broadcasted_iota(jnp.int32, (PAD_ROWS, rows), 0)
    own_place = (d * 32 + t) * rows + lax.broadcasted_iota(jnp.int32, (PAD_ROWS, rows), 1)
    last_pick = jnp.zeros((PAD_ROWS, rows), F32)
    start = jnp.int32(0)
    for r in range(lengths.shape[0]):
        slot = adapter_slot[request_adapter[r]]
        slots = jnp.where(place >= start, slot, slots)
        start = start + lengths[r]
        last_pick = jnp.where((pick_at == r) & (own_place == start - 1), 1.0, last_pick)
    slots = slots.astype(F32)
    for p in range(4):
        slot_grid[p] = jnp.transpose(jnp.broadcast_to(slots[p : p + 1], (rows, rows)))

    pl.semaphore_wait(barrier, len(greeted))

    def meta_copy(p):
        return pltpu.make_async_remote_copy(
            src_ref=meta.at[0],
            dst_ref=meta.at[p],
            send_sem=meta_send_sem.at[p],
            recv_sem=meta_recv_sem.at[p],
            device_id=along_first(HOPS[p]),
            device_id_type=MESH,
        )

    def first_copy(p):
        return pltpu.make_async_remote_copy(
            src_ref=first_rows.at[0],
            dst_ref=first_rows.at[p],
            send_sem=first_send_sem.at[p],
            recv_sem=first_recv_sem.at[p],
            device_id=along_first(HOPS[p]),
            device_id_type=MESH,
        )

    def peer_copy(p):
        return pltpu.make_async_remote_copy(
            src_ref=peer_rows.at[0],
            dst_ref=peer_rows.at[p],
            send_sem=peer_send_sem.at[p],
            recv_sem=peer_recv_sem.at[p],
            device_id=along_x(HOPS[p]),
            device_id_type=MESH,
        )

    for p in (1, 2, 3):
        meta_copy(p).start()
        first_copy(p).start()
    for p in (1, 2, 3):
        peer_copy(p).start()

    def pick_copy(p, j):
        return pltpu.make_async_remote_copy(
            src_ref=picked.at[p, j],
            dst_ref=arrived.at[p, own_q],
            send_sem=pick_send_sem.at[p, j],
            recv_sem=pick_recv_sem.at[p, own_q],
            device_id=(d, expert_of(j)),
            device_id_type=MESH,
        )

    def pick_wait(p, q):
        return pltpu.make_async_remote_copy(
            src_ref=picked.at[p, own_j],
            dst_ref=arrived.at[p, q],
            send_sem=pick_send_sem.at[p, own_j],
            recv_sem=pick_recv_sem.at[p, q],
            device_id=(d, relay_of(q)),
            device_id_type=MESH,
        )

    def own_at(q):
        return jnp.where(q < 4, z * 2 + c, y * 2 + c)

    def ret_copy(p, q):
        return pltpu.make_async_remote_copy(
            src_ref=results.at[p, q],
            dst_ref=returned.at[p, own_at(q)],
            send_sem=ret_send_sem.at[p, q],
            recv_sem=ret_recv_sem.at[p, own_at(q)],
            device_id=(d, relay_of(q)),
            device_id_type=MESH,
        )

    def ret_wait(p, j):
        return pltpu.make_async_remote_copy(
            src_ref=results.at[p, own_q],
            dst_ref=returned.at[p, j],
            send_sem=ret_send_sem.at[p, own_q],
            recv_sem=ret_recv_sem.at[p, j],
            device_id=(d, expert_of(j)),
            device_id_type=MESH,
        )

    def other_j(r):
        near = ((1, 0), (3, 0), (1, 1), (3, 1), (2, 0), (2, 1), (0, 1))[r]
        return ((own_j // 2 + near[0]) % 4) * 2 + (c + near[1]) % 2

    def other_q(r):
        return (own_q + r + 1) % 8

    tri_a = lax.broadcasted_iota(jnp.int32, (rows, rows), 0)
    tri_b = lax.broadcasted_iota(jnp.int32, (rows, rows), 1)
    upper = jnp.where(tri_a <= tri_b, 1.0, 0.0).astype(F32)
    index_j = lax.broadcasted_iota(jnp.int32, (8, rows), 0)
    wanted = expert_of(index_j).astype(F32)
    slot_index = lax.broadcasted_iota(jnp.int32, (8, CAP, rows), 1).astype(F32)

    def select(p):
        table = meta[p]
        chosen = jnp.zeros((8, rows), F32)
        weight = jnp.zeros((8, rows), F32)
        for k in range(6):
            same = table[k : k + 1, :] == wanted
            chosen = jnp.where(same, 1.0, chosen)
            weight = jnp.where(same, table[8 + k : 9 + k, :], weight)
        count = jnp.dot(chosen, upper, preferred_element_type=F32)
        slot_of = jnp.where(chosen > 0.5, count - 1.0, -1.0)
        hit = jnp.broadcast_to(slot_of[:, None, :], (8, CAP, rows)) == slot_index
        pick = jnp.where(hit, 1.0, 0.0).reshape(8 * CAP, rows).astype(BF16)
        mix = jnp.where(hit, jnp.broadcast_to(weight[:, None, :], (8, CAP, rows)), 0.0)
        mixing[p] = jnp.transpose(mix.reshape(8 * CAP, rows)).astype(BF16)

        def columns(n, carry):
            cols = pl.ds(pl.multiple_of(n * 512, 512), 512)
            got = jnp.dot(pick, first_rows[p, :, cols], preferred_element_type=F32)
            picked[p, :, :, cols] = got.astype(BF16).reshape(8, CAP, 512)
            return carry

        lax.fori_loop(0, width // 512, columns, 0)
        arrived[p, own_q] = picked[p, own_j]
        for r in range(7):
            pick_copy(p, other_j(r)).start()

    def shared(b):
        at_b = pl.ds(b * 2, 2)
        x = peer_rows[at_b].reshape(2 * rows, width)
        gate_part = dot_rows(x, w_sgate[...])
        up_part = dot_rows(x, w_sup[...])
        inner = (gate_part / (1.0 + jnp.exp(-gate_part)) * up_part).astype(BF16)
        low = dot_rows(x, w_ldown[...])
        lanes = lax.broadcasted_iota(jnp.int32, low.shape, 1) // 16 + d * 8
        keep = slot_grid[at_b].reshape(2 * rows, rows) == lanes.astype(F32)
        low = jnp.where(keep, low, 0.0).astype(BF16)

        def columns(n, carry):
            cols = pl.ds(pl.multiple_of(n * 512, 512), 512)
            part = jnp.dot(inner, w_sdown[:, cols], preferred_element_type=F32)
            part = part + jnp.dot(low, w_lup[:, cols], preferred_element_type=F32)
            shared_send[at_b, :, cols] = part.astype(BF16).reshape(2, rows, 512)

            @pl.when(b == 0)
            def _():
                total[:, cols] = part[:rows]

            return carry

        lax.fori_loop(0, width // 512, columns, 0)

    def shared_copy(p):
        return pltpu.make_async_remote_copy(
            src_ref=shared_send.at[p],
            dst_ref=shared_recv.at[p],
            send_sem=shared_send_sem.at[p],
            recv_sem=shared_recv_sem.at[p],
            device_id=along_x(4 - HOPS[p]),
            device_id_type=MESH,
        )

    def part_copy(p, hop):
        return pltpu.make_async_remote_copy(
            src_ref=part_send.at[p],
            dst_ref=part_recv.at[p],
            send_sem=part_send_sem.at[p],
            recv_sem=part_recv_sem.at[p],
            device_id=along_first(4 - hop),
            device_id_type=MESH,
        )

    inner_width = w_gate.shape[1]
    wide = inner_width // 256

    def gated(p, cols):
        x = arrived[p].reshape(8 * CAP, width)
        gate_part = jnp.dot(x, w_gate[:, cols], preferred_element_type=F32)
        up_part = jnp.dot(x, w_up[:, cols], preferred_element_type=F32)
        act = gate_part / (1.0 + jnp.exp(-gate_part)) * up_part
        hidden[:, cols] = act.astype(BF16)

    def expert(p):
        for r in range(7):
            pick_wait(p, other_q(r)).wait_recv()

        def columns(n, carry):
            gated(p, pl.ds(pl.multiple_of(n * 256, 256), 256))
            return carry

        lax.fori_loop(0, wide, columns, 0)
        if inner_width > wide * 256:
            gated(p, pl.ds(wide * 256, inner_width - wide * 256))

        def down(n, carry):
            cols = pl.ds(pl.multiple_of(n * 512, 512), 512)
            got = jnp.dot(hidden[...], w_down[:, cols], preferred_element_type=F32)
            results[p, :, :, cols] = got.astype(BF16).reshape(8, CAP, 512)
            return carry

        lax.fori_loop(0, width // 512, down, 0)
        returned[p, own_j] = results[p, own_q]
        for r in range(7):
            ret_copy(p, other_q(r)).start()

    def combine(p, own):
        for r in range(7):
            ret_wait(p, other_j(r)).wait_recv()

        def columns(n, carry):
            cols = pl.ds(pl.multiple_of(n * 512, 512), 512)
            got = jnp.dot(
                mixing[p],
                returned[p, :, :, cols].reshape(8 * CAP, 512),
                preferred_element_type=F32,
            )
            if own:
                total[:, cols] += got
            else:
                part_send[p, :, cols] = got.astype(BF16)
            return carry

        lax.fori_loop(0, width // 512, columns, 0)

    def select_step(i, carry):
        p = (i + 1) % 4

        @pl.when(p > 0)
        def _():
            pltpu.make_async_remote_copy(
                src_ref=meta.at[0],
                dst_ref=meta.at[p],
                send_sem=meta_send_sem.at[p],
                recv_sem=meta_recv_sem.at[p],
                device_id=along_first(1),
                device_id_type=MESH,
            ).wait_recv()
            pltpu.make_async_remote_copy(
                src_ref=first_rows.at[0],
                dst_ref=first_rows.at[p],
                send_sem=first_send_sem.at[p],
                recv_sem=first_recv_sem.at[p],
                device_id=along_first(1),
                device_id_type=MESH,
            ).wait_recv()

        select(p)
        return carry

    lax.fori_loop(0, 4, select_step, 0)

    for load in loads[:5]:
        load.wait()
    peer_copy(1).wait_recv()

    def shared_step(b, carry):
        @pl.when(b == 1)
        def _():
            peer_copy(2).wait_recv()
            peer_copy(3).wait_recv()

        shared(b)
        return carry

    for load in loads[5:8]:
        load.wait()

    def combine_step(p):
        combine(p, False)
        part_copy(p, jnp.where(p == 2, 3, jnp.where(p == 3, 2, p))).start()

    def expert_step(i, carry):
        expert((i + 1) % 4)

        @pl.when(i < 2)
        def _():
            shared_step(i, 0)

            @pl.when(i == 0)
            def _():
                shared_copy(1).start()

            @pl.when(i == 1)
            def _():
                shared_copy(2).start()
                shared_copy(3).start()

        @pl.when(i > 1)
        def _():
            combine_step(i - 1)

        return carry

    lax.fori_loop(0, 4, expert_step, 0)
    combine_step(3)
    combine(0, True)

    for p in (1, 2, 3):
        shared_copy(p).wait_recv()
    for p in (1, 2, 3):
        part_copy(p, HOPS[p]).wait_recv()

    def finish(n, carry):
        cols = pl.ds(pl.multiple_of(n * 512, 512), 512)
        value = total[:, cols]
        for p in (1, 2, 3):
            value = value + shared_recv[p, :, cols].astype(F32)
            value = value + part_recv[p, :, cols].astype(F32)
        out[:, cols] = value.astype(BF16)
        return carry

    lax.fori_loop(0, width // 512, finish, 0)

    half = width // 2
    pick_last = last_pick.astype(BF16)
    for h in (0, 1):
        mine = jnp.dot(pick_last, out[:, h * half : (h + 1) * half], preferred_element_type=F32)
        last_mine[h] = mine.astype(BF16)

    def core_copy(i, src, dst):
        return pltpu.make_async_remote_copy(
            src_ref=src,
            dst_ref=dst,
            send_sem=core_send_sem.at[i],
            recv_sem=core_recv_sem.at[i],
            device_id=at(y, z, 1 - c),
            device_id_type=MESH,
        )

    swap = core_copy(0, last_mine.at[1 - c], last_core)
    swap.start()
    swap.wait_recv()
    last_sum[0] = (last_mine[c].astype(F32) + last_core[...].astype(F32)).astype(BF16)
    stage_copies = []
    third = half // 384 * 128
    groups = ((0, third), (third, third), (2 * third, half - 2 * third))
    for a in range(3):
        copies = []
        for k in (1, 3, 2):
            for g, (off, size) in enumerate(groups):
                targets = (at(y, (z + k) % 4, c), at((y + k) % 4, z, c), along_x(k))
                copies.append(
                    pltpu.make_async_remote_copy(
                        src_ref=last_sum.at[a, :, pl.ds(off, size)],
                        dst_ref=last_recv.at[a, k, :, pl.ds(off, size)],
                        send_sem=last_send_sem.at[a, g, k],
                        recv_sem=last_recv_sem.at[a, g, k],
                        device_id=targets[(a + g) % 3],
                        device_id_type=MESH,
                    )
                )
        for copy in copies:
            copy.start()
        for copy in copies:
            copy.wait_recv()
        value = last_sum[a].astype(F32)
        for k in (1, 2, 3):
            value = value + last_recv[a, k].astype(F32)
        last_sum[a + 1] = value.astype(BF16)
        stage_copies += copies
    last_full[c] = last_sum[3]
    spread = core_copy(1, last_sum.at[3], last_full.at[c])
    spread.start()
    loads[8].wait()
    spread.wait_recv()

    square = jnp.zeros((PAD_ROWS, 1), F32)
    logits = jnp.zeros((PAD_ROWS, w_head.shape[1]), F32)
    for h in (0, 1):
        value = last_full[h]
        wide_value = value.astype(F32)
        square = square + jnp.sum(wide_value * wide_value, axis=1, keepdims=True)
        logits = logits + jnp.dot(
            value, w_head[h * half : (h + 1) * half, :], preferred_element_type=F32
        )
    requests = norm_out.shape[0]
    norms = jnp.transpose(jnp.broadcast_to(jnp.sqrt(square), top_mine.shape))
    norm_out[...] = norms[:1, :requests].reshape(requests)
    best = jnp.max(logits, axis=1, keepdims=True)
    top_mine[...] = jnp.broadcast_to(best, top_mine.shape)
    top_copies = []
    for k in (1, 3, 2):
        top_copies.append(
            pltpu.make_async_remote_copy(
                src_ref=top_mine,
                dst_ref=top_recv.at[k],
                send_sem=top_send_sem.at[k],
                recv_sem=top_recv_sem.at[k],
                device_id=along_x(k),
                device_id_type=MESH,
            )
        )
    for copy in top_copies:
        copy.start()
    for copy in top_copies:
        copy.wait_recv()
    best = top_mine[...]
    for k in (1, 2, 3):
        best = jnp.maximum(best, top_recv[k])
    logit_out[...] = jnp.transpose(best)[:1, :requests]

    for p in (1, 2, 3):
        meta_copy(p).wait_send()
        first_copy(p).wait_send()
        peer_copy(p).wait_send()
        shared_copy(p).wait_send()
        part_copy(p, HOPS[p]).wait_send()

    def drain(p, carry):
        for r in range(7):
            pick_copy(p, other_j(r)).wait_send()
            ret_copy(p, other_q(r)).wait_send()
        return carry

    lax.fori_loop(0, 4, drain, 0)
    swap.wait_send()
    spread.wait_send()
    for copy in stage_copies + top_copies:
        copy.wait_send()


def local(
    tokens,
    norm_gain,
    routes,
    route_gates,
    lengths,
    request_adapter,
    adapter_slot,
    expert_gate,
    expert_up,
    expert_down,
    shared_gate,
    shared_up_weight,
    shared_down,
    adapter_down,
    adapter_up,
    head_weight,
):
    rows, width = tokens.shape
    inner_width = expert_gate.shape[2]
    shared_width = shared_gate.shape[1]
    held, _, rank = adapter_down.shape
    columns = head_weight.shape[1]
    requests = lengths.shape[0]
    low_down = jnp.transpose(adapter_down, (0, 2, 1)).reshape(held * rank, width)
    low_up = adapter_up.reshape(held * rank, width)
    vmem = pl.BlockSpec(memory_space=pltpu.VMEM)
    smem = pl.BlockSpec(memory_space=pltpu.SMEM)
    anywhere = pl.BlockSpec(memory_space=pl.ANY)
    dma = pltpu.SemaphoreType.DMA
    half = width // 2
    sublayer, last_norm, block_logit = pl.pallas_call(
        body,
        out_shape=(
            jax.ShapeDtypeStruct((rows, width), BF16),
            jax.ShapeDtypeStruct((requests,), F32),
            jax.ShapeDtypeStruct((1, requests), F32),
        ),
        in_specs=[smem] * 3 + [vmem] * 4 + [anywhere] * 9,
        out_specs=(vmem, vmem, vmem),
        scratch_shapes=[
            pltpu.VMEM((width, inner_width), BF16),
            pltpu.VMEM((width, inner_width), BF16),
            pltpu.VMEM((inner_width, width), BF16),
            pltpu.VMEM((shared_width, width), BF16),
            pltpu.VMEM((shared_width, width), BF16),
            pltpu.VMEM((shared_width, width), BF16),
            pltpu.VMEM((held * rank, width), BF16),
            pltpu.VMEM((held * rank, width), BF16),
            pltpu.VMEM((width, columns), BF16),
            pltpu.VMEM((4, rows, width), BF16),
            pltpu.VMEM((4, rows, width), BF16),
            pltpu.VMEM((4, 16, rows), F32),
            pltpu.VMEM((4, 8, CAP, width), BF16),
            pltpu.VMEM((4, 8, CAP, width), BF16),
            pltpu.VMEM((4, 8, CAP, width), BF16),
            pltpu.VMEM((4, 8, CAP, width), BF16),
            pltpu.VMEM((4, rows, 8 * CAP), BF16),
            pltpu.VMEM((8 * CAP, inner_width), BF16),
            pltpu.VMEM((4, rows, width), BF16),
            pltpu.VMEM((4, rows, width), BF16),
            pltpu.VMEM((4, rows, width), BF16),
            pltpu.VMEM((4, rows, width), BF16),
            pltpu.VMEM((rows, width), F32),
            pltpu.VMEM((4, rows, rows), F32),
            pltpu.VMEM((2, PAD_ROWS, half), BF16),
            pltpu.VMEM((PAD_ROWS, half), BF16),
            pltpu.VMEM((4, PAD_ROWS, half), BF16),
            pltpu.VMEM((3, 4, PAD_ROWS, half), BF16),
            pltpu.VMEM((2, PAD_ROWS, half), BF16),
            pltpu.VMEM((PAD_ROWS, 128), F32),
            pltpu.VMEM((4, PAD_ROWS, 128), F32),
            dma((9,)),
            dma((4,)),
            dma((4,)),
            dma((4,)),
            dma((4,)),
            dma((4,)),
            dma((4,)),
            dma((4, 8)),
            dma((4, 8)),
            dma((4, 8)),
            dma((4, 8)),
            dma((4,)),
            dma((4,)),
            dma((4,)),
            dma((4,)),
            dma((2,)),
            dma((2,)),
            dma((3, 3, 4)),
            dma((3, 3, 4)),
            dma((4,)),
            dma((4,)),
        ],
        compiler_params=pltpu.CompilerParams(
            collective_id=0, has_side_effects=True, vmem_limit_bytes=63 << 20
        ),
        name="sublayer",
    )(
        lengths,
        request_adapter,
        adapter_slot,
        tokens,
        norm_gain,
        routes.T,
        route_gates.T,
        expert_gate,
        expert_up,
        expert_down,
        shared_gate.T,
        shared_up_weight.T,
        shared_down,
        low_down,
        low_up,
        head_weight,
    )
    return (sublayer, last_norm, block_logit.T)


def solution(mesh):
    placed = (
        P(("dp", "tensor"), None),
        P(),
        P(("dp", "tensor"), None),
        P(("dp", "tensor"), None),
        P(),
        P(),
        P(),
        P("tensor", None, None),
        P("tensor", None, None),
        P("tensor", None, None),
        P(None, "dp"),
        P(None, "dp"),
        P("dp", None),
        P("dp", None, None),
        P("dp", None, None),
        P(None, ("dp", "tensor")),
    )
    return jax.shard_map(
        local,
        mesh=mesh,
        in_specs=placed,
        out_specs=(P(("dp", "tensor"), None), P(), P(None, "tensor")),
        check_vma=False,
    )
```

```python
import functools

import jax
import jax.numpy as jnp
from jax import lax
from jax.experimental import pallas as pl
from jax.experimental.pallas import tpu as pltpu
from jax.sharding import PartitionSpec as P

CAP = 32
HOPS = (0, 1, 3, 2)
PAD_ROWS = 32
F32 = jnp.float32
BF16 = jnp.bfloat16
MESH = pl.DeviceIdType.MESH


def dot_rows(a, b):
    return lax.dot_general(a, b, (((1,), (1,)), ((), ())), preferred_element_type=F32)


def body(
    lengths,
    request_adapter,
    adapter_slot,
    tokens,
    gain,
    routes_in,
    gates_in,
    expert_gate,
    expert_up,
    expert_down,
    shared_gate,
    shared_up,
    shared_down,
    low_down,
    low_up,
    head,
    out,
    norm_out,
    logit_out,
    w_gate,
    w_up,
    w_down,
    w_sgate,
    w_sup,
    w_sdown,
    w_ldown,
    w_lup,
    w_head,
    first_rows,
    peer_rows,
    meta,
    picked,
    arrived,
    results,
    returned,
    mixing,
    hidden,
    part_send,
    part_recv,
    shared_send,
    shared_recv,
    total,
    slot_grid,
    last_mine,
    last_core,
    last_sum,
    last_recv,
    last_full,
    top_mine,
    top_recv,
    load_sem,
    meta_send_sem,
    meta_recv_sem,
    first_send_sem,
    first_recv_sem,
    peer_send_sem,
    peer_recv_sem,
    pick_send_sem,
    pick_recv_sem,
    ret_send_sem,
    ret_recv_sem,
    part_send_sem,
    part_recv_sem,
    shared_send_sem,
    shared_recv_sem,
    core_send_sem,
    core_recv_sem,
    last_send_sem,
    last_recv_sem,
    top_send_sem,
    top_recv_sem,
):
    width = tokens.shape[1]
    rows = tokens.shape[0]
    d = lax.axis_index("dp")
    t = lax.axis_index("tensor")
    y = t // 8
    z = (t // 2) % 4
    c = t % 2
    one = c == 1

    def at(ty, tz, tc):
        return (d, ty * 8 + tz * 2 + tc)

    def along_first(k):
        return at(
            jnp.where(one, y, (y + k) % 4),
            jnp.where(one, (z + k) % 4, z),
            c,
        )

    def along_x(k):
        return ((d + k) % 4, t)

    def expert_of(j):
        return jnp.where(one, (j // 2) * 8 + z * 2 + j % 2, y * 8 + j)

    own_j = jnp.where(one, y * 2 + 1, z * 2)
    own_q = jnp.where(one, 4 + y, z)

    def relay_of(q):
        return jnp.where(q < 4, y * 8 + q * 2, (q - 4) * 8 + z * 2 + 1)

    loads = []
    for i, (src, dst) in enumerate(
        (
            (shared_gate, w_sgate),
            (shared_up, w_sup),
            (low_down, w_ldown),
            (shared_down, w_sdown),
            (low_up, w_lup),
            (expert_gate.at[0], w_gate),
            (expert_up.at[0], w_up),
            (expert_down.at[0], w_down),
            (head, w_head),
        )
    ):
        loads.append(pltpu.make_async_copy(src, dst, load_sem.at[i]))
    for load in loads:
        load.start()

    barrier = pltpu.get_barrier_semaphore()
    greeted = [at(y, z, 1 - c)]
    for k in (1, 2, 3):
        for o in (0, 1):
            greeted.append(at(y, (z + k) % 4, o))
            greeted.append(at((y + k) % 4, z, o))
        greeted.append(along_x(k))
    for target in greeted:
        pl.semaphore_signal(barrier, inc=1, device_id=target, device_id_type=MESH)

    values = tokens[...].astype(F32)
    scaled = lax.rsqrt(jnp.mean(values * values, axis=-1, keepdims=True) + 1e-06)
    gains = gain[...].astype(F32).reshape(1, width)
    normed = (values * scaled * gains).astype(BF16)
    first_rows[0] = normed
    peer_rows[0] = normed
    meta[0] = jnp.zeros_like(meta[0])
    meta[0, 0:6] = routes_in[...].astype(F32)
    meta[0, 8:14] = gates_in[...].astype(F32)

    lane = lax.broadcasted_iota(jnp.int32, (8, rows), 1)
    row = lax.broadcasted_iota(jnp.int32, (8, rows), 0)
    hop = jnp.where(row == 2, 3, jnp.where(row == 3, 2, row))
    place = (((d - hop + 8) % 4) * 32 + t) * rows + lane
    slots = jnp.zeros((8, rows), jnp.int32)
    pick_at = lax.broadcasted_iota(jnp.int32, (PAD_ROWS, rows), 0)
    own_place = (d * 32 + t) * rows + lax.broadcasted_iota(jnp.int32, (PAD_ROWS, rows), 1)
    last_pick = jnp.zeros((PAD_ROWS, rows), F32)
    start = jnp.int32(0)
    for r in range(lengths.shape[0]):
        slot = adapter_slot[request_adapter[r]]
        slots = jnp.where(place >= start, slot, slots)
        start = start + lengths[r]
        last_pick = jnp.where((pick_at == r) & (own_place == start - 1), 1.0, last_pick)
    slots = slots.astype(F32)
    for p in range(4):
        slot_grid[p] = jnp.transpose(jnp.broadcast_to(slots[p : p + 1], (rows, rows)))

    pl.semaphore_wait(barrier, len(greeted))

    def meta_copy(p):
        return pltpu.make_async_remote_copy(
            src_ref=meta.at[0],
            dst_ref=meta.at[p],
            send_sem=meta_send_sem.at[p],
            recv_sem=meta_recv_sem.at[p],
            device_id=along_first(HOPS[p]),
            device_id_type=MESH,
        )

    def first_copy(p):
        return pltpu.make_async_remote_copy(
            src_ref=first_rows.at[0],
            dst_ref=first_rows.at[p],
            send_sem=first_send_sem.at[p],
            recv_sem=first_recv_sem.at[p],
            device_id=along_first(HOPS[p]),
            device_id_type=MESH,
        )

    def peer_copy(p):
        return pltpu.make_async_remote_copy(
            src_ref=peer_rows.at[0],
            dst_ref=peer_rows.at[p],
            send_sem=peer_send_sem.at[p],
            recv_sem=peer_recv_sem.at[p],
            device_id=along_x(HOPS[p]),
            device_id_type=MESH,
        )

    for p in (1, 2, 3):
        meta_copy(p).start()
        first_copy(p).start()
    for p in (1, 2, 3):
        peer_copy(p).start()

    def pick_copy(p, j):
        return pltpu.make_async_remote_copy(
            src_ref=picked.at[p, j],
            dst_ref=arrived.at[p, own_q],
            send_sem=pick_send_sem.at[p, j],
            recv_sem=pick_recv_sem.at[p, own_q],
            device_id=(d, expert_of(j)),
            device_id_type=MESH,
        )

    def pick_wait(p, q):
        return pltpu.make_async_remote_copy(
            src_ref=picked.at[p, own_j],
            dst_ref=arrived.at[p, q],
            send_sem=pick_send_sem.at[p, own_j],
            recv_sem=pick_recv_sem.at[p, q],
            device_id=(d, relay_of(q)),
            device_id_type=MESH,
        )

    def own_at(q):
        return jnp.where(q < 4, z * 2 + c, y * 2 + c)

    def ret_copy(p, q):
        return pltpu.make_async_remote_copy(
            src_ref=results.at[p, q],
            dst_ref=returned.at[p, own_at(q)],
            send_sem=ret_send_sem.at[p, q],
            recv_sem=ret_recv_sem.at[p, own_at(q)],
            device_id=(d, relay_of(q)),
            device_id_type=MESH,
        )

    def ret_wait(p, j):
        return pltpu.make_async_remote_copy(
            src_ref=results.at[p, own_q],
            dst_ref=returned.at[p, j],
            send_sem=ret_send_sem.at[p, own_q],
            recv_sem=ret_recv_sem.at[p, j],
            device_id=(d, expert_of(j)),
            device_id_type=MESH,
        )

    def other_j(r):
        near = ((1, 0), (3, 0), (1, 1), (3, 1), (2, 0), (2, 1), (0, 1))[r]
        return ((own_j // 2 + near[0]) % 4) * 2 + (c + near[1]) % 2

    def other_q(r):
        return (own_q + r + 1) % 8

    tri_a = lax.broadcasted_iota(jnp.int32, (rows, rows), 0)
    tri_b = lax.broadcasted_iota(jnp.int32, (rows, rows), 1)
    upper = jnp.where(tri_a <= tri_b, 1.0, 0.0).astype(F32)
    index_j = lax.broadcasted_iota(jnp.int32, (8, rows), 0)
    wanted = expert_of(index_j).astype(F32)
    slot_index = lax.broadcasted_iota(jnp.int32, (8, CAP, rows), 1).astype(F32)

    def select(p):
        table = meta[p]
        chosen = jnp.zeros((8, rows), F32)
        weight = jnp.zeros((8, rows), F32)
        for k in range(6):
            same = table[k : k + 1, :] == wanted
            chosen = jnp.where(same, 1.0, chosen)
            weight = jnp.where(same, table[8 + k : 9 + k, :], weight)
        count = jnp.dot(chosen, upper, preferred_element_type=F32)
        slot_of = jnp.where(chosen > 0.5, count - 1.0, -1.0)
        hit = jnp.broadcast_to(slot_of[:, None, :], (8, CAP, rows)) == slot_index
        pick = jnp.where(hit, 1.0, 0.0).reshape(8 * CAP, rows).astype(BF16)
        mix = jnp.where(hit, jnp.broadcast_to(weight[:, None, :], (8, CAP, rows)), 0.0)
        mixing[p] = jnp.transpose(mix.reshape(8 * CAP, rows)).astype(BF16)

        def columns(n, carry):
            cols = pl.ds(pl.multiple_of(n * 512, 512), 512)
            got = jnp.dot(pick, first_rows[p, :, cols], preferred_element_type=F32)
            picked[p, :, :, cols] = got.astype(BF16).reshape(8, CAP, 512)
            return carry

        lax.fori_loop(0, width // 512, columns, 0)
        arrived[p, own_q] = picked[p, own_j]
        for r in range(7):
            pick_copy(p, other_j(r)).start()

    def shared(b):
        at_b = pl.ds(b * 2, 2)
        x = peer_rows[at_b].reshape(2 * rows, width)
        gate_part = dot_rows(x, w_sgate[...])
        up_part = dot_rows(x, w_sup[...])
        inner = (gate_part / (1.0 + jnp.exp(-gate_part)) * up_part).astype(BF16)
        low = dot_rows(x, w_ldown[...])
        lanes = lax.broadcasted_iota(jnp.int32, low.shape, 1) // 16 + d * 8
        keep = slot_grid[at_b].reshape(2 * rows, rows) == lanes.astype(F32)
        low = jnp.where(keep, low, 0.0).astype(BF16)

        def columns(n, carry):
            cols = pl.ds(pl.multiple_of(n * 512, 512), 512)
            part = jnp.dot(inner, w_sdown[:, cols], preferred_element_type=F32)
            part = part + jnp.dot(low, w_lup[:, cols], preferred_element_type=F32)
            shared_send[at_b, :, cols] = part.astype(BF16).reshape(2, rows, 512)

            @pl.when(b == 0)
            def _():
                total[:, cols] = part[:rows]

            return carry

        lax.fori_loop(0, width // 512, columns, 0)

    def shared_copy(p):
        return pltpu.make_async_remote_copy(
            src_ref=shared_send.at[p],
            dst_ref=shared_recv.at[p],
            send_sem=shared_send_sem.at[p],
            recv_sem=shared_recv_sem.at[p],
            device_id=along_x(4 - HOPS[p]),
            device_id_type=MESH,
        )

    def part_copy(p, hop):
        return pltpu.make_async_remote_copy(
            src_ref=part_send.at[p],
            dst_ref=part_recv.at[p],
            send_sem=part_send_sem.at[p],
            recv_sem=part_recv_sem.at[p],
            device_id=along_first(4 - hop),
            device_id_type=MESH,
        )

    inner_width = w_gate.shape[1]
    wide = inner_width // 256

    def gated(p, cols):
        x = arrived[p].reshape(8 * CAP, width)
        gate_part = jnp.dot(x, w_gate[:, cols], preferred_element_type=F32)
        up_part = jnp.dot(x, w_up[:, cols], preferred_element_type=F32)
        act = gate_part / (1.0 + jnp.exp(-gate_part)) * up_part
        hidden[:, cols] = act.astype(BF16)

    def expert(p):
        for r in range(7):
            pick_wait(p, other_q(r)).wait_recv()

        def columns(n, carry):
            gated(p, pl.ds(pl.multiple_of(n * 256, 256), 256))
            return carry

        lax.fori_loop(0, wide, columns, 0)
        if inner_width > wide * 256:
            gated(p, pl.ds(wide * 256, inner_width - wide * 256))

        def down(n, carry):
            cols = pl.ds(pl.multiple_of(n * 512, 512), 512)
            got = jnp.dot(hidden[...], w_down[:, cols], preferred_element_type=F32)
            results[p, :, :, cols] = got.astype(BF16).reshape(8, CAP, 512)
            return carry

        lax.fori_loop(0, width // 512, down, 0)
        returned[p, own_j] = results[p, own_q]
        for r in range(7):
            ret_copy(p, other_q(r)).start()

    def combine(p, own):
        for r in range(7):
            ret_wait(p, other_j(r)).wait_recv()

        def columns(n, carry):
            cols = pl.ds(pl.multiple_of(n * 512, 512), 512)
            got = jnp.dot(
                mixing[p],
                returned[p, :, :, cols].reshape(8 * CAP, 512),
                preferred_element_type=F32,
            )
            if own:
                total[:, cols] += got
            else:
                part_send[p, :, cols] = got.astype(BF16)
            return carry

        lax.fori_loop(0, width // 512, columns, 0)

    def select_step(i, carry):
        p = (i + 1) % 4

        @pl.when(p > 0)
        def _():
            pltpu.make_async_remote_copy(
                src_ref=meta.at[0],
                dst_ref=meta.at[p],
                send_sem=meta_send_sem.at[p],
                recv_sem=meta_recv_sem.at[p],
                device_id=along_first(1),
                device_id_type=MESH,
            ).wait_recv()
            pltpu.make_async_remote_copy(
                src_ref=first_rows.at[0],
                dst_ref=first_rows.at[p],
                send_sem=first_send_sem.at[p],
                recv_sem=first_recv_sem.at[p],
                device_id=along_first(1),
                device_id_type=MESH,
            ).wait_recv()

        select(p)
        return carry

    lax.fori_loop(0, 4, select_step, 0)

    for load in loads[:5]:
        load.wait()
    peer_copy(1).wait_recv()

    def shared_step(b, carry):
        @pl.when(b == 1)
        def _():
            peer_copy(2).wait_recv()
            peer_copy(3).wait_recv()

        shared(b)
        return carry

    for load in loads[5:8]:
        load.wait()

    def combine_step(p):
        combine(p, False)
        part_copy(p, jnp.where(p == 2, 3, jnp.where(p == 3, 2, p))).start()

    def expert_step(i, carry):
        expert((i + 1) % 4)

        @pl.when(i < 2)
        def _():
            shared_step(i, 0)

            @pl.when(i == 0)
            def _():
                shared_copy(1).start()

            @pl.when(i == 1)
            def _():
                shared_copy(2).start()
                shared_copy(3).start()

        return carry

    lax.fori_loop(0, 4, expert_step, 0)

    def combine_all(p, carry):
        combine_step(p)
        return carry

    lax.fori_loop(1, 4, combine_all, 0)
    combine(0, True)

    for p in (1, 2, 3):
        shared_copy(p).wait_recv()
    for p in (1, 2, 3):
        part_copy(p, HOPS[p]).wait_recv()

    def finish(n, carry):
        cols = pl.ds(pl.multiple_of(n * 512, 512), 512)
        value = total[:, cols]
        for p in (1, 2, 3):
            value = value + shared_recv[p, :, cols].astype(F32)
            value = value + part_recv[p, :, cols].astype(F32)
        out[:, cols] = value.astype(BF16)
        return carry

    lax.fori_loop(0, width // 512, finish, 0)

    half = width // 2
    pick_last = last_pick.astype(BF16)
    for h in (0, 1):
        mine = jnp.dot(pick_last, out[:, h * half : (h + 1) * half], preferred_element_type=F32)
        last_mine[h] = mine.astype(BF16)

    def core_copy(i, src, dst):
        return pltpu.make_async_remote_copy(
            src_ref=src,
            dst_ref=dst,
            send_sem=core_send_sem.at[i],
            recv_sem=core_recv_sem.at[i],
            device_id=at(y, z, 1 - c),
            device_id_type=MESH,
        )

    swap = core_copy(0, last_mine.at[1 - c], last_core)
    swap.start()
    swap.wait_recv()
    last_sum[0] = (last_mine[c].astype(F32) + last_core[...].astype(F32)).astype(BF16)
    stage_copies = []
    third = half // 384 * 128
    groups = ((0, third), (third, third), (2 * third, half - 2 * third))
    for a in range(3):
        copies = []
        for k in (1, 3, 2):
            for g, (off, size) in enumerate(groups):
                targets = (at(y, (z + k) % 4, c), at((y + k) % 4, z, c), along_x(k))
                copies.append(
                    pltpu.make_async_remote_copy(
                        src_ref=last_sum.at[a, :, pl.ds(off, size)],
                        dst_ref=last_recv.at[a, k, :, pl.ds(off, size)],
                        send_sem=last_send_sem.at[a, g, k],
                        recv_sem=last_recv_sem.at[a, g, k],
                        device_id=targets[(a + g) % 3],
                        device_id_type=MESH,
                    )
                )
        for copy in copies:
            copy.start()
        for copy in copies:
            copy.wait_recv()
        value = last_sum[a].astype(F32)
        for k in (1, 2, 3):
            value = value + last_recv[a, k].astype(F32)
        last_sum[a + 1] = value.astype(BF16)
        stage_copies += copies
    last_full[c] = last_sum[3]
    spread = core_copy(1, last_sum.at[3], last_full.at[c])
    spread.start()
    loads[8].wait()
    spread.wait_recv()

    square = jnp.zeros((PAD_ROWS, 1), F32)
    logits = jnp.zeros((PAD_ROWS, w_head.shape[1]), F32)
    for h in (0, 1):
        value = last_full[h]
        wide_value = value.astype(F32)
        square = square + jnp.sum(wide_value * wide_value, axis=1, keepdims=True)
        logits = logits + jnp.dot(
            value, w_head[h * half : (h + 1) * half, :], preferred_element_type=F32
        )
    requests = norm_out.shape[0]
    norms = jnp.transpose(jnp.broadcast_to(jnp.sqrt(square), top_mine.shape))
    norm_out[...] = norms[:1, :requests].reshape(requests)
    best = jnp.max(logits, axis=1, keepdims=True)
    top_mine[...] = jnp.broadcast_to(best, top_mine.shape)
    top_copies = []
    for k in (1, 3, 2):
        top_copies.append(
            pltpu.make_async_remote_copy(
                src_ref=top_mine,
                dst_ref=top_recv.at[k],
                send_sem=top_send_sem.at[k],
                recv_sem=top_recv_sem.at[k],
                device_id=along_x(k),
                device_id_type=MESH,
            )
        )
    for copy in top_copies:
        copy.start()
    for copy in top_copies:
        copy.wait_recv()
    best = top_mine[...]
    for k in (1, 2, 3):
        best = jnp.maximum(best, top_recv[k])
    logit_out[...] = jnp.transpose(best)[:1, :requests]

    for p in (1, 2, 3):
        meta_copy(p).wait_send()
        first_copy(p).wait_send()
        peer_copy(p).wait_send()
        shared_copy(p).wait_send()
        part_copy(p, HOPS[p]).wait_send()

    def drain(p, carry):
        for r in range(7):
            pick_copy(p, other_j(r)).wait_send()
            ret_copy(p, other_q(r)).wait_send()
        return carry

    lax.fori_loop(0, 4, drain, 0)
    swap.wait_send()
    spread.wait_send()
    for copy in stage_copies + top_copies:
        copy.wait_send()


def local(
    tokens,
    norm_gain,
    routes,
    route_gates,
    lengths,
    request_adapter,
    adapter_slot,
    expert_gate,
    expert_up,
    expert_down,
    shared_gate,
    shared_up_weight,
    shared_down,
    adapter_down,
    adapter_up,
    head_weight,
):
    rows, width = tokens.shape
    inner_width = expert_gate.shape[2]
    shared_width = shared_gate.shape[1]
    held, _, rank = adapter_down.shape
    columns = head_weight.shape[1]
    requests = lengths.shape[0]
    low_down = jnp.transpose(adapter_down, (0, 2, 1)).reshape(held * rank, width)
    low_up = adapter_up.reshape(held * rank, width)
    vmem = pl.BlockSpec(memory_space=pltpu.VMEM)
    smem = pl.BlockSpec(memory_space=pltpu.SMEM)
    anywhere = pl.BlockSpec(memory_space=pl.ANY)
    dma = pltpu.SemaphoreType.DMA
    half = width // 2
    sublayer, last_norm, block_logit = pl.pallas_call(
        body,
        out_shape=(
            jax.ShapeDtypeStruct((rows, width), BF16),
            jax.ShapeDtypeStruct((requests,), F32),
            jax.ShapeDtypeStruct((1, requests), F32),
        ),
        in_specs=[smem] * 3 + [vmem] * 4 + [anywhere] * 9,
        out_specs=(vmem, vmem, vmem),
        scratch_shapes=[
            pltpu.VMEM((width, inner_width), BF16),
            pltpu.VMEM((width, inner_width), BF16),
            pltpu.VMEM((inner_width, width), BF16),
            pltpu.VMEM((shared_width, width), BF16),
            pltpu.VMEM((shared_width, width), BF16),
            pltpu.VMEM((shared_width, width), BF16),
            pltpu.VMEM((held * rank, width), BF16),
            pltpu.VMEM((held * rank, width), BF16),
            pltpu.VMEM((width, columns), BF16),
            pltpu.VMEM((4, rows, width), BF16),
            pltpu.VMEM((4, rows, width), BF16),
            pltpu.VMEM((4, 16, rows), F32),
            pltpu.VMEM((4, 8, CAP, width), BF16),
            pltpu.VMEM((4, 8, CAP, width), BF16),
            pltpu.VMEM((4, 8, CAP, width), BF16),
            pltpu.VMEM((4, 8, CAP, width), BF16),
            pltpu.VMEM((4, rows, 8 * CAP), BF16),
            pltpu.VMEM((8 * CAP, inner_width), BF16),
            pltpu.VMEM((4, rows, width), BF16),
            pltpu.VMEM((4, rows, width), BF16),
            pltpu.VMEM((4, rows, width), BF16),
            pltpu.VMEM((4, rows, width), BF16),
            pltpu.VMEM((rows, width), F32),
            pltpu.VMEM((4, rows, rows), F32),
            pltpu.VMEM((2, PAD_ROWS, half), BF16),
            pltpu.VMEM((PAD_ROWS, half), BF16),
            pltpu.VMEM((4, PAD_ROWS, half), BF16),
            pltpu.VMEM((3, 4, PAD_ROWS, half), BF16),
            pltpu.VMEM((2, PAD_ROWS, half), BF16),
            pltpu.VMEM((PAD_ROWS, 128), F32),
            pltpu.VMEM((4, PAD_ROWS, 128), F32),
            dma((9,)),
            dma((4,)),
            dma((4,)),
            dma((4,)),
            dma((4,)),
            dma((4,)),
            dma((4,)),
            dma((4, 8)),
            dma((4, 8)),
            dma((4, 8)),
            dma((4, 8)),
            dma((4,)),
            dma((4,)),
            dma((4,)),
            dma((4,)),
            dma((2,)),
            dma((2,)),
            dma((3, 3, 4)),
            dma((3, 3, 4)),
            dma((4,)),
            dma((4,)),
        ],
        compiler_params=pltpu.CompilerParams(
            collective_id=0, has_side_effects=True, vmem_limit_bytes=63 << 20
        ),
        name="sublayer",
    )(
        lengths,
        request_adapter,
        adapter_slot,
        tokens,
        norm_gain,
        routes.T,
        route_gates.T,
        expert_gate,
        expert_up,
        expert_down,
        shared_gate.T,
        shared_up_weight.T,
        shared_down,
        low_down,
        low_up,
        head_weight,
    )
    return (sublayer, last_norm, block_logit.T)


def solution(mesh):
    placed = (
        P(("dp", "tensor"), None),
        P(),
        P(("dp", "tensor"), None),
        P(("dp", "tensor"), None),
        P(),
        P(),
        P(),
        P("tensor", None, None),
        P("tensor", None, None),
        P("tensor", None, None),
        P(None, "dp"),
        P(None, "dp"),
        P("dp", None),
        P("dp", None, None),
        P("dp", None, None),
        P(None, ("dp", "tensor")),
    )
    return jax.shard_map(
        local,
        mesh=mesh,
        in_specs=placed,
        out_specs=(P(("dp", "tensor"), None), P(), P(None, "tensor")),
        check_vma=False,
    )
```
